512 devices in a mesh: dp: 64 (over x, z), expert: 8 (over y, core).
Axes of the slice: x: 4, y: 4, z: 16, core: 2. Of those that a mesh axis runs over, the one named last changes fastest.
Arguments:
- grad_out: bfloat16 [131072, 1024], P(('dp', 'expert')), may hold values from -1 to 1
- routes: int32 [131072, 6], P(('dp', 'expert')), may hold values from 0 to 63, all different within a row; in each aligned block of 256 rows (0 to 255, 256 to 511, ...) at most 48 rows name the same one
- route_weight: float32 [131072, 6], P(('dp', 'expert')), may hold values from 0.05 to 0.35
- example_ids: int32 [64, 2048], P('dp', 'expert'), may hold values from 0 to 7, never falling along the last dimension, each value on 1 to 512 neighbouring positions
- example_weight: float32 [64, 8], P('dp'), may hold values from 0.5 to 50
- hidden: bfloat16 [64, 8, 8, 48, 704], P('dp', 'expert'), may hold values from -6 to 6
Outputs:
- expert_grads: float32 [704, 8, 1024], P('dp', 'expert')
The draws below stay inside these ranges and needn't reach their ends.
Inputs may be any that keep to these rules, and one draw needn't show every extreme that they name: `routes`: each row names 6 different experts; in the rows of one device no expert is named more than 48 times, a bound that some block reaches. `example_ids`: along a data group's tokens the numbers never fall; each of the 8 examples has from 1 to a quarter of 2048 tokens, one exactly that many.
All inputs are finite; a program needn't handle non-finite values.
Results may differ from the reference program's by a relative error of at most 0.0011.
Values may be sent and summed in bfloat16 or wider, within the bound.
A program may use at most 64 MiB of HBM per device.

```python
import math
import jax
import jax.numpy as jnp
import numpy as np
from jax import lax

EXPERTS = 64
TOP = 6
FF_WIN = 704
D_WIN = 1024
EXAMPLES = 8
TOK_DEV = 256
SOURCES = 8
EXP_FLIGHT = 8
GROUPS = 64
GROUP_TOK = 2048
TOKENS = 131072
CAP = 48
N_DP = 64


def draw_grad_out(key, part):
    own_key, common_key = jax.random.split(jax.random.fold_in(key, 101), 2)
    own = jax.random.normal(own_key, (GROUPS, GROUP_TOK, D_WIN), jnp.float32)
    common = 0.7 * jax.random.normal(common_key, (GROUPS, 1, D_WIN), jnp.float32)
    values = own + common
    values = jnp.clip(values / math.sqrt(TOK_DEV), -1.0, 1.0)
    return values.reshape(TOKENS, D_WIN).astype(jnp.bfloat16)


def draw_hidden(key, part):
    own_key, common_key = jax.random.split(jax.random.fold_in(key, 202), 2)
    own = jax.random.normal(own_key, (GROUPS, EXP_FLIGHT, SOURCES, CAP, FF_WIN), jnp.float32)
    common = 0.7 * jax.random.normal(common_key, (GROUPS, EXP_FLIGHT, 1, 1, FF_WIN), jnp.float32)
    values = own + common
    return jnp.clip(values, -6.0, 6.0).astype(jnp.bfloat16)


def block_levels(key, extent, shards, least, top_value):
    factor_of = 1.0
    for axis_at, blocks in shards:
        heights = jax.random.uniform(jax.random.fold_in(jax.random.fold_in(key, 6), axis_at), (blocks,), jnp.float32, least / len(shards), top_value / len(shards))
        factor_of = factor_of * jnp.repeat(jnp.exp(heights), extent[axis_at] // blocks).reshape((-1,) + (1,) * (len(extent) - 1 - axis_at))
    return factor_of


def split_up(amount, total, most, skew):
    loads = [(1 << 20) // math.isqrt(grade ** skew) + 1 for grade in range(2, amount + 1)]
    spare, holding = total - most - (amount - 1), [1] * (amount - 1)
    while spare > 0:
        movable = [i for i in range(amount - 1) if holding[i] < most]
        pool, budget = sum([loads[i] for i in movable]), spare
        for i in movable:
            extra = min(most - holding[i], max(1, budget * loads[i] // pool), spare)
            holding[i] = holding[i] + extra
            spare = spare - extra
    return np.array([most] + holding)


def ragged_sizes(key, count, total, most, slope):
    if count == 2:
        one = jax.random.randint(key, (), max(1, total - most), min(most, total - 1) + 1)
        return jnp.stack([one, total - one])
    sizes = jnp.asarray(split_up(count, total, most, slope), jnp.int32)
    twos = (count - 1) // 2
    giver, sink = sizes[1:1 + 2 * twos:2], sizes[2:2 + 2 * twos:2]
    room = jnp.minimum(giver - 1, most - sink)
    passed = jax.random.randint(jax.random.fold_in(key, 1), (twos,), 0, 1 << 20) % (room + 1)
    sizes = sizes.at[1:1 + 2 * twos:2].set(giver - passed).at[2:2 + 2 * twos:2].set(sink + passed)
    return sizes[jax.random.permutation(jax.random.fold_in(key, 2), count)]


def deal_out(key, own, number, rows, count, top, reach, skew):
    order = jax.random.permutation(key, count)
    packed, usual = load_shares(count, rows * top, reach, skew, True), load_shares(count, rows * top, reach, skew, False)
    places = jnp.arange(count)

    def named(lengths, turn):
        used = int((lengths > 0).sum())
        fixed = max(1, used // 4)
        shifted = fixed + (places - fixed + turn * (used - fixed)) % max(1, count - fixed)
        return jnp.zeros((count,), jnp.int32).at[order[jnp.where(places < fixed, places, shifted)]].set(jnp.asarray(lengths, jnp.int32))

    lengths = jnp.where(number % 4 == 0, named(packed, number // 4), named(usual, number - number // 4 - 1))
    mixed = jax.random.permutation(jax.random.fold_in(own, 3), count)
    source_of, sink = mixed[0:count // 2 * 2:2], mixed[1:count // 2 * 2:2]
    margin = jnp.minimum(lengths[source_of] - 1, reach - lengths[sink]) // 2
    margin = jnp.where((source_of == order[0]) | (sink == order[0]) | (lengths[sink] == 0), 0, jnp.maximum(margin, 0))
    shifted = jax.random.randint(jax.random.fold_in(own, 4), (count // 2,), 0, 1 << 20) % (margin + 1)
    lengths = lengths.at[source_of].add(-shifted).at[sink].add(shifted)
    labels = jnp.searchsorted(jnp.cumsum(lengths), jnp.arange(rows * top), side="right").astype(jnp.int32)
    listing = labels.reshape(top, rows).T
    listing = listing[jax.random.permutation(jax.random.fold_in(own, 1), rows)]
    turn = jax.random.randint(jax.random.fold_in(own, 2), (rows, 1), 0, top)
    return jnp.take_along_axis(listing, (jnp.arange(top)[None, :] + turn) % top, axis=1)


def load_shares(number_of, total, limit, lean, full):
    portions = [(1 << 20) // math.isqrt(rank ** lean) + 1 for rank in range(1, number_of + 1)]
    largest = limit if full else min(limit, max(-(-total // number_of), total * portions[0] // sum(portions)))
    least = 1 if total - largest >= number_of - 1 else 0
    counts, rest = [largest] + [least] * (number_of - 1), total - largest - least * (number_of - 1)
    while rest > 0:
        free = [i for i in range(1, number_of) if counts[i] < largest] or [i for i in range(1, number_of) if counts[i] < limit]
        pool, left = sum([portions[i] for i in free]), rest
        for i in free:
            addition = min(limit - counts[i], max(1, left * portions[i] // pool), rest)
            counts[i] = counts[i] + addition
            rest = rest - addition
    return np.array(counts)


def setup_inputs(seed: int = 0) -> dict:
    key_of = jax.random.split(jax.random.key(seed), 7)
    grad_out = draw_grad_out(jax.random.fold_in(key_of[6], 71), 0)
    routes_keys = jax.random.split(jax.random.fold_in(key_of[1], 1), TOKENS // TOK_DEV)
    routes_turns = jax.random.permutation(jax.random.fold_in(key_of[1], 3), TOKENS // TOK_DEV)
    routes = jax.vmap(lambda own, number: deal_out(jax.random.fold_in(key_of[1], 2), own, number, TOK_DEV, EXPERTS, TOP, CAP, 2))(routes_keys, routes_turns).reshape((TOKENS, TOP))
    route_weight = jnp.clip(0.05 + 0.29999999 * jax.random.uniform(key_of[2], (TOKENS, TOP), jnp.float32) ** block_levels(key_of[2], (TOKENS, TOP), ((0, 512),), -0.2, 0.2), 0.05, 0.35)
    example_ids = jax.vmap(lambda own: jnp.searchsorted(jnp.cumsum(ragged_sizes(own, EXAMPLES, GROUP_TOK, GROUP_TOK // 4, 0)), jnp.arange(GROUP_TOK), side="right"))(jax.random.split(key_of[3], GROUPS)).reshape((GROUPS, GROUP_TOK)).astype(jnp.int32)
    example_weight = jnp.clip(jnp.exp(math.log(50.0) - 4.6051702 * jax.random.uniform(key_of[4], (GROUPS, EXAMPLES), jnp.float32) ** block_levels(key_of[4], (GROUPS, EXAMPLES), ((0, 64),), -0.2, 0.2)), 0.5, 50.0)
    hidden = draw_hidden(jax.random.fold_in(key_of[6], 71), 0)
    return dict(grad_out=grad_out, routes=routes, route_weight=route_weight, example_ids=example_ids, example_weight=example_weight, hidden=hidden)


def slot_layout(block_routes, expert_list, capacity):
    matches = (block_routes[..., None] == expert_list).astype(jnp.float32)
    routed = lax.optimization_barrier(jnp.sum(matches, axis=-2))
    ranking = jnp.cumsum(routed, axis=-2) - routed
    slot_index = jnp.arange(capacity).astype(jnp.float32)
    placed = routed[..., None] * (ranking[..., None] == slot_index).astype(jnp.float32)
    return (matches, placed)

def reference(grad_out, routes, route_weight, example_ids, example_weight, hidden):
    highest = lax.Precision.HIGHEST
    in_flight = jnp.arange(EXP_FLIGHT).astype(jnp.int32)
    example_index = jnp.arange(EXAMPLES).astype(jnp.int32)
    cot_groups = grad_out.reshape(N_DP, SOURCES, TOK_DEV, D_WIN)
    route_groups = routes.reshape(N_DP, SOURCES, TOK_DEV, TOP)
    weight_groups = route_weight.reshape(N_DP, SOURCES, TOK_DEV, TOP)
    id_groups = example_ids.reshape(N_DP, SOURCES, TOK_DEV)

    def per_group(running, group_data):
        cot_rows, route_rows, weight_rows, id_rows, loss_weights, acts_group = group_data
        matches, placed = slot_layout(route_rows, in_flight, CAP)
        membership = (id_rows[..., None] == example_index).astype(jnp.float32)
        token_weight = lax.optimization_barrier(jnp.sum(membership * loss_weights, axis=-1))
        token_scale = lax.optimization_barrier(jnp.sum(matches * weight_rows[..., None], axis=-2)) * token_weight[..., None]
        slot_rows = jnp.einsum('stec,std->escd', placed, cot_rows.astype(jnp.float32), precision=highest)
        slot_scale = jnp.transpose(lax.optimization_barrier(jnp.sum(placed * token_scale[..., None], axis=1)), (1, 0, 2))
        slot_cot = (slot_rows * slot_scale[..., None]).astype(jnp.bfloat16)
        cot_flat = slot_cot.reshape(EXP_FLIGHT, SOURCES * CAP, D_WIN).astype(jnp.float32)
        member = jnp.einsum('stec,stx->escx', placed, membership, precision=highest).reshape(EXP_FLIGHT, SOURCES * CAP, EXAMPLES)
        acts_flat = acts_group.reshape(EXP_FLIGHT, SOURCES * CAP, FF_WIN).astype(jnp.float32)
        gram_left = jnp.einsum('eif,ekf->eik', acts_flat, acts_flat, precision=highest)
        gram_right = jnp.einsum('eid,ekd->eik', cot_flat, cot_flat, precision=highest)
        spread = jnp.einsum('eik,ekx->eix', gram_left * gram_right, member, precision=highest)
        squares = lax.optimization_barrier(jnp.sum(spread * member, axis=(0, 1)))
        clip_factor = 1.0 / jnp.maximum(jnp.sqrt(squares / (FF_WIN * D_WIN)), 1.0)
        slot_weight = lax.optimization_barrier(jnp.sum(member * clip_factor, axis=-1)) / EXAMPLES
        scaled = (slot_weight[..., None] * cot_flat).astype(jnp.bfloat16).astype(jnp.float32)
        group_grads = jnp.einsum('eif,eid->fed', acts_flat, scaled, precision=highest)
        return (running + group_grads, None)
    summed_grads, unused_out = lax.scan(per_group, jnp.zeros((FF_WIN, EXP_FLIGHT, D_WIN), jnp.float32), (cot_groups, route_groups, weight_groups, id_groups, example_weight, hidden))
    return summed_grads
```

```python
import functools

import jax
import jax.numpy as jnp
from jax import lax
from jax.experimental import pallas as pl
from jax.experimental.pallas import tpu as pltpu
from jax.sharding import PartitionSpec as P

EXAMPLES = 8
TOP = 6
NX = 4
MESH = pl.DeviceIdType.MESH
F32 = jnp.float32
BF16 = jnp.bfloat16

REL = ((2, 0), (2, 1), (1, 0), (3, 0), (1, 1), (3, 1), (0, 1), (0, 0))


def nt_dot(a, b):
    return lax.dot_general(a, b, (((1,), (1,)), ((), ())), preferred_element_type=F32)


def nn_dot(a, b):
    return lax.dot_general(a, b, (((1,), (0,)), ((), ())), preferred_element_type=F32)


def iota(shape, dim):
    return lax.broadcasted_iota(jnp.int32, shape, dim)


def other(src, dst, send_sem, recv_sem, **device):
    return pltpu.make_async_remote_copy(
        src_ref=src, dst_ref=dst, send_sem=send_sem, recv_sem=recv_sem,
        device_id=device, device_id_type=MESH,
    )


def body(
    cfg,
    go_ref, routes_ref, weight_ref, ids_ref, ew_ref, h_ref,
    out_ref,
    h_buf, rank_s, scale_s, lo_s, hi_s, send_buf, c_buf, meta_send, meta_recv, sq_send, sq_recv,
    gl_s, ht_s, scaled_s,
    acc_a, ax_opp, ax_dir, azp, azm,
    h_sem, c_send, c_recv, m_send, m_recv, q_send, q_recv,
    ax_send, ax_recv, azp_send, azp_recv, azm_send, azm_recv,
):
    nz, ff, dw, cap, tok = cfg
    half_ring = nz // 2
    dp, me = lax.axis_index("dp"), lax.axis_index("expert")
    x, z = dp // nz, dp % nz
    y, core = me // 2, me % 2
    xp, xm, x2 = (x + 1) % NX, (x + 3) % NX, (x + 2) % NX
    zp, zm = (z + 1) % nz, (z + nz - 1) % nz
    at_xp, at_xm = dict(dp=xp * nz + z), dict(dp=xm * nz + z)
    at_zp, at_zm = dict(dp=x * nz + zp), dict(dp=x * nz + zm)
    dest = [((y + dy) % 4) * 2 + (core + dc) % 2 for dy, dc in REL]
    source = [((y + 4 - dy) % 4) * 2 + (core + 2 - dc) % 2 for dy, dc in REL]

    barrier = pltpu.get_barrier_semaphore()
    for p in range(7):
        pl.semaphore_signal(barrier, inc=1, device_id={"expert": dest[p]}, device_id_type=MESH)
    for place in (at_xp, at_xm, at_zp, at_zm):
        pl.semaphore_signal(barrier, inc=1, device_id=place, device_id_type=MESH)

    h_copies = [
        pltpu.make_async_copy(h_ref.at[source[p]], h_buf.at[p], h_sem.at[p]) for p in range(8)
    ]
    for copy in h_copies:
        copy.start()

    expert_row = iota((8, tok), 0)
    routed = jnp.zeros((8, tok), F32)
    weight = jnp.zeros((8, tok), F32)
    for k in range(TOP):
        match = routes_ref[k : k + 1, :] == expert_row
        routed = jnp.where(match, 1.0, routed)
        weight = jnp.where(match, weight_ref[k : k + 1, :], weight)
    ids = ids_ref[...]
    token_weight = jnp.zeros((1, tok), F32)
    for example in range(EXAMPLES):
        token_weight = jnp.where(
            ids == example, ew_ref[0:1, example : example + 1], token_weight
        )
    earlier = (iota((tok, tok), 0) < iota((tok, tok), 1)).astype(F32).astype(BF16)
    routed_b = routed.astype(BF16)
    rank = nn_dot(routed_b, earlier)
    rank_s[...] = jnp.where(routed > 0.5, rank, -1.0)
    scale_s[...] = weight * token_weight
    example_col = iota((128, tok), 0)
    lo_s[...] = nt_dot(routed_b, (ids < example_col).astype(F32).astype(BF16))
    hi_s[...] = nt_dot(routed_b, (ids <= example_col).astype(F32).astype(BF16))

    slot_col = iota((cap, tok), 0).astype(F32)
    sub8 = iota((8, 128), 0)
    c_copies, m_copies = [], []
    for p in range(7):
        c_copies.append(
            other(send_buf.at[p], c_buf.at[p], c_send.at[p], c_recv.at[p], expert=dest[p])
        )
        m_copies.append(
            other(meta_send.at[p], meta_recv.at[p], m_send.at[p], m_recv.at[p], expert=dest[p])
        )
    for batch in ((0, 1, 2, 3), (4, 5, 6, 7)):
        masks, scales = [], []
        for p in batch:
            hit = rank_s[pl.ds(dest[p], 1), :] == slot_col
            masks.append(hit.astype(F32).astype(BF16))
            scales.append(
                jnp.sum(jnp.where(hit, scale_s[pl.ds(dest[p], 1), :], 0.0), axis=1, keepdims=True)
            )
        rows = nn_dot(jnp.concatenate(masks, axis=0), go_ref[...])
        if batch[0] == 0:
            pl.semaphore_wait(barrier, 11)
        for i, p in enumerate(batch):
            value = (rows[i * cap : (i + 1) * cap, :] * scales[i]).astype(BF16)
            bounds = jnp.where(
                sub8 == 0, lo_s[pl.ds(dest[p], 1), :], hi_s[pl.ds(dest[p], 1), :]
            )
            if p == 7:
                c_buf[7] = value
                meta_recv[7] = bounds
            else:
                send_buf[p] = value
                meta_send[p] = bounds
                c_copies[p].start()
                m_copies[p].start()

    for copy in h_copies:
        copy.wait()
    h = h_buf[...].reshape(8 * cap, ff)
    gl_s[...] = nt_dot(h, h)
    eye = (iota((ff, ff), 0) == iota((ff, ff), 1)).astype(F32).astype(BF16)
    ht_s[...] = nt_dot(eye, h).astype(BF16)

    for p in range(7):
        m_copies[p].wait_recv()
    slot_128 = iota((cap, 128), 0).astype(F32)
    member = jnp.concatenate(
        [
            jnp.where(
                (slot_128 >= meta_recv[p, 0:1, :]) & (slot_128 < meta_recv[p, 1:2, :]), 1.0, 0.0
            )
            for p in range(8)
        ],
        axis=0,
    )
    member_b = member.astype(BF16)
    gl_s[...] = gl_s[...] * nt_dot(member_b, member_b)
    for p in range(7):
        c_copies[p].wait_recv()
    cot = c_buf[...].reshape(8 * cap, dw)
    spread = jnp.sum(gl_s[...] * nt_dot(cot, cot), axis=1, keepdims=True)
    squares = jnp.sum(member * spread, axis=0, keepdims=True)
    sq_send[...] = jnp.broadcast_to(squares, (8, 128))
    q_copies = [
        other(sq_send, sq_recv.at[p], q_send.at[p], q_recv.at[p], expert=dest[p]) for p in range(7)
    ]
    for copy in q_copies:
        copy.start()
    total = squares
    for p in range(7):
        q_copies[p].wait_recv()
        total = total + sq_recv[p, 0:1, :]
    clip = 1.0 / jnp.maximum(jnp.sqrt(total / (ff * dw)), 1.0)
    slot_weight = jnp.sum(member * clip, axis=1, keepdims=True) / EXAMPLES
    scaled_s[...] = (slot_weight * cot.astype(F32)).astype(BF16)

    rows_x = ff // NX
    t = rows_x // nz * (dw // 128)
    half = half_ring * t

    def gradient(chunk):
        start = pl.multiple_of(chunk * rows_x, 16)
        value = nn_dot(ht_s[pl.ds(start, rows_x), :], scaled_s[...])
        for j in range(dw // 128):
            acc_a[chunk, pl.ds(j, rows_x, stride=dw // 128), :] = value[:, j * 128 : (j + 1) * 128]

    lower, upper = pl.ds(0, half), pl.ds(half, half)
    gradient(x2)
    opp = [
        other(acc_a.at[x2, lower], ax_opp.at[0], ax_send.at[0], ax_recv.at[0], **at_xp),
        other(acc_a.at[x2, upper], ax_opp.at[1], ax_send.at[1], ax_recv.at[1], **at_xm),
    ]
    for copy in opp:
        copy.start()
    first = [
        other(acc_a.at[xp, upper], ax_dir.at[0, upper], ax_send.at[2], ax_recv.at[2], **at_xp),
        other(acc_a.at[xm, lower], ax_dir.at[1, lower], ax_send.at[3], ax_recv.at[3], **at_xm),
    ]
    gradient(xp)
    first[0].start()
    gradient(xm)
    first[1].start()
    gradient(x)
    second = [
        other(acc_a.at[xp, lower], ax_dir.at[0, lower], ax_send.at[4], ax_recv.at[4], **at_xp),
        other(acc_a.at[xm, upper], ax_dir.at[1, upper], ax_send.at[5], ax_recv.at[5], **at_xm),
    ]
    opp[0].wait_recv()
    acc_a[xp, lower, :] = acc_a[xp, lower, :] + ax_opp[0]
    second[0].start()
    opp[1].wait_recv()
    acc_a[xm, upper, :] = acc_a[xm, upper, :] + ax_opp[1]
    second[1].start()
    for copy in first + second:
        copy.wait_recv()
    acc_a[x] = acc_a[x] + (ax_dir[0] + ax_dir[1])

    def rows_of(d):
        return pl.ds(pl.multiple_of(d * t, 8), t)

    ring = []
    for step in range(half_ring):
        d = rows_of((z + half_ring - step) % nz)
        if step:
            ring[-1][0].wait_recv()
            acc_a[x, d, :] = acc_a[x, d, :] + azp[step - 1]
        pair = [
            other(acc_a.at[x, d], azp.at[step], azp_send.at[step], azp_recv.at[step], **at_zp)
        ]
        pair[0].start()
        if step < half_ring - 1:
            d = rows_of((z + nz - (half_ring - 1) + step) % nz)
            if step:
                ring[-1][1].wait_recv()
                acc_a[x, d, :] = acc_a[x, d, :] + azm[step - 1]
            pair.append(
                other(acc_a.at[x, d], azm.at[step], azm_send.at[step], azm_recv.at[step], **at_zm)
            )
            pair[1].start()
        ring.append(pair)
    ring[half_ring - 2][1].wait_recv()
    ring[half_ring - 1][0].wait_recv()
    out_ref[...] = acc_a[x, rows_of(z), :] + azp[half_ring - 1] + azm[half_ring - 2]
    for copy in c_copies + m_copies + q_copies + opp + first + second + [c for p in ring for c in p]:
        copy.wait_send()


def shards(nz, grad_out, routes, route_weight, example_ids, example_weight, hidden):
    tok, dw = grad_out.shape
    cap, ff = hidden.shape[3:]
    rows_x = ff // NX * (dw // 128)
    t = rows_x // nz
    half_ring = nz // 2
    dma = pltpu.SemaphoreType.DMA
    vmem = pl.BlockSpec(memory_space=pltpu.VMEM)
    scratch = [
        pltpu.VMEM((8, cap, ff), BF16),
        pltpu.VMEM((8, tok), F32),
        pltpu.VMEM((8, tok), F32),
        pltpu.VMEM((8, 128), F32),
        pltpu.VMEM((8, 128), F32),
        pltpu.VMEM((7, cap, dw), BF16),
        pltpu.VMEM((8, cap, dw), BF16),
        pltpu.VMEM((7, 8, 128), F32),
        pltpu.VMEM((8, 8, 128), F32),
        pltpu.VMEM((8, 128), F32),
        pltpu.VMEM((7, 8, 128), F32),
        pltpu.VMEM((8 * cap, 8 * cap), F32),
        pltpu.VMEM((ff, 8 * cap), BF16),
        pltpu.VMEM((8 * cap, dw), BF16),
        pltpu.VMEM((NX, rows_x, 128), F32),
        pltpu.VMEM((2, rows_x // 2, 128), F32),
        pltpu.VMEM((2, rows_x, 128), F32),
        pltpu.VMEM((half_ring, t, 128), F32),
        pltpu.VMEM((max(half_ring - 1, 1), t, 128), F32),
        dma((8,)), dma((7,)), dma((7,)), dma((7,)), dma((7,)), dma((7,)), dma((7,)),
        dma((6,)), dma((6,)), dma((half_ring,)), dma((half_ring,)), dma((half_ring,)), dma((half_ring,)),
    ]
    out = pl.pallas_call(
        functools.partial(body, (nz, ff, dw, cap, tok)),
        out_shape=jax.ShapeDtypeStruct((t, 128), F32),
        in_specs=[vmem] * 5 + [pl.BlockSpec(memory_space=pl.ANY)],
        out_specs=vmem,
        scratch_shapes=scratch,
        compiler_params=pltpu.CompilerParams(
            collective_id=0, has_side_effects=True, vmem_limit_bytes=48 * 1024 * 1024
        ),
        name="clipped_grads",
    )(grad_out, routes.T, route_weight.T, example_ids, example_weight, hidden[0, 0])
    return out.reshape(t // (dw // 128), 1, dw)


def solution(mesh):
    nz = mesh.shape["dp"] // NX
    placed = (
        P(("dp", "expert"), None),
        P(("dp", "expert"), None),
        P(("dp", "expert"), None),
        P("dp", "expert"),
        P("dp", None),
        P("dp", "expert", None, None, None),
    )
    return jax.shard_map(
        functools.partial(shards, nz), mesh=mesh, in_specs=placed,
        out_specs=P("dp", "expert", None), check_vma=False,
    )
```

```python
import functools

import jax
import jax.numpy as jnp
from jax import lax
from jax.experimental import pallas as pl
from jax.experimental.pallas import tpu as pltpu
from jax.sharding import PartitionSpec as P

EXAMPLES = 8
TOP = 6
NX = 4
MESH = pl.DeviceIdType.MESH
F32 = jnp.float32
BF16 = jnp.bfloat16

X_FIRST = 6
LINKS = 112

REL = ((2, 0), (2, 1), (1, 0), (3, 0), (1, 1), (3, 1), (0, 1), (0, 0))


def nt_dot(a, b):
    return lax.dot_general(a, b, (((1,), (1,)), ((), ())), preferred_element_type=F32)


def nn_dot(a, b):
    return lax.dot_general(a, b, (((1,), (0,)), ((), ())), preferred_element_type=F32)


def iota(shape, dim):
    return lax.broadcasted_iota(jnp.int32, shape, dim)


def other(src, dst, send_sem, recv_sem, **device):
    return pltpu.make_async_remote_copy(
        src_ref=src, dst_ref=dst, send_sem=send_sem, recv_sem=recv_sem,
        device_id=device, device_id_type=MESH,
    )


def encode(value):
    most = jnp.max(jnp.abs(value), axis=0, keepdims=True)
    step = jnp.maximum(most, 1e-33) * (1.0 / 32760.0)
    code = jnp.round(value * (1.0 / step)).astype(jnp.int32)
    return code, jnp.broadcast_to(step, (8, 128))


def decode(code, step):
    return code.astype(jnp.int32).astype(F32) * step


def body(
    cfg,
    go_hbm, routes_hbm, weight_hbm, ids_hbm, ew_hbm, h_ref,
    out_ref,
    go_ref, routes_ref, weight_ref, ids_ref, ew_ref,
    h_buf, rank_s, scale_s, lo_s, hi_s, send_buf, relay_buf, c_buf, meta_send, meta_recv, sq_send, sq_recv,
    gl_s, ht_s, scaled_s,
    acc_a, acc_b, x_codes, x_steps, x_in, x_in_steps,
    za_codes, za_in, zb_codes, zb_in, za2_codes, za2_in, zb2_codes, zb2_in,
    z_steps, z_in_steps, bx_codes, bx_in, bx_steps,
    local_sem, send_sem, recv_sem,
):
    nz, ff, dw, cap, tok = cfg
    lanes = dw // 128
    dp, me = lax.axis_index("dp"), lax.axis_index("expert")
    x, z = dp // nz, dp % nz
    y, core = me // 2, me % 2
    xp, xm, x2 = (x + 1) % NX, (x + 3) % NX, (x + 2) % NX

    def expert_at(dy, dc):
        return dict(expert=((y + dy) % 4) * 2 + (core + dc) % 2)

    def x_at(dx):
        return dict(dp=((x + dx) % NX) * nz + z)

    def z_at(dz):
        return dict(dp=x * nz + (z + nz + dz) % nz)

    dest = [expert_at(dy, dc)["expert"] for dy, dc in REL]
    source = [((y + 4 - dy) % 4) * 2 + (core + 2 - dc) % 2 for dy, dc in REL]
    copies = []

    def link(src, dst, place):
        n = len(copies)
        copies.append(other(src, dst, send_sem.at[n], recv_sem.at[n], **place))
        return copies[-1]

    barrier = pltpu.get_barrier_semaphore()
    greeted = [expert_at(dy, dc) for dy, dc in REL[:7]]
    greeted += [x_at(dx) for dx in (1, 2, 3)] + [z_at(dz) for dz in (1, -1, 2, -2, 3, -3, 5, -5)]
    for place in greeted:
        pl.semaphore_signal(barrier, inc=1, device_id=place, device_id_type=MESH)

    inputs = [
        pltpu.make_async_copy(src, dst, local_sem.at[n])
        for n, (src, dst) in enumerate((
            (routes_hbm, routes_ref), (weight_hbm, weight_ref), (ids_hbm, ids_ref),
            (ew_hbm, ew_ref), (go_hbm, go_ref),
        ))
    ]
    for copy in inputs:
        copy.start()
    h_copies = [
        pltpu.make_async_copy(h_ref.at[source[p]], h_buf.at[p], local_sem.at[5 + p])
        for p in range(8)
    ]
    for copy in h_copies:
        copy.start()
    for copy in inputs[:4]:
        copy.wait()

    expert_row = iota((8, tok), 0)
    routed = jnp.zeros((8, tok), F32)
    weight = jnp.zeros((8, tok), F32)
    for k in range(TOP):
        match = routes_ref[k : k + 1, :] == expert_row
        routed = jnp.where(match, 1.0, routed)
        weight = jnp.where(match, weight_ref[k : k + 1, :], weight)
    ids = ids_ref[...]
    token_weight = jnp.zeros((1, tok), F32)
    for example in range(EXAMPLES):
        token_weight = jnp.where(
            ids == example, ew_ref[0:1, example : example + 1], token_weight
        )
    earlier = (iota((tok, tok), 0) < iota((tok, tok), 1)).astype(F32).astype(BF16)
    routed_b = routed.astype(BF16)
    rank = nn_dot(routed_b, earlier)
    rank_s[...] = jnp.where(routed > 0.5, rank, -1.0)
    scale_s[...] = weight * token_weight
    example_col = iota((128, tok), 0)
    lo_s[...] = nt_dot(routed_b, (ids < example_col).astype(F32).astype(BF16))
    hi_s[...] = nt_dot(routed_b, (ids <= example_col).astype(F32).astype(BF16))

    slot_col = iota((cap, tok), 0).astype(F32)
    sub8 = iota((8, 128), 0)
    c_copies = [
        link(send_buf.at[0], relay_buf.at[0], expert_at(1, 0)),
        link(send_buf.at[1], relay_buf.at[1], expert_at(3, 0)),
    ]
    c_copies += [link(send_buf.at[p], c_buf.at[p], expert_at(*REL[p])) for p in range(2, 7)]
    relays = [
        link(relay_buf.at[0], c_buf.at[0], expert_at(1, 0)),
        link(relay_buf.at[1], c_buf.at[1], expert_at(3, 1)),
    ]
    m_copies = [link(meta_send.at[p], meta_recv.at[p], expert_at(*REL[p])) for p in range(7)]
    inputs[4].wait()
    for batch in ((0, 1), (2, 3, 4, 5), (6, 7)):
        masks, scales = [], []
        for p in batch:
            hit = rank_s[pl.ds(dest[p], 1), :] == slot_col
            masks.append(hit.astype(F32).astype(BF16))
            scales.append(
                jnp.sum(jnp.where(hit, scale_s[pl.ds(dest[p], 1), :], 0.0), axis=1, keepdims=True)
            )
        rows = nn_dot(jnp.concatenate(masks, axis=0), go_ref[...])
        if batch[0] == 0:
            pl.semaphore_wait(barrier, len(greeted))
        for i, p in enumerate(batch):
            value = (rows[i * cap : (i + 1) * cap, :] * scales[i]).astype(BF16)
            bounds = jnp.where(
                sub8 == 0, lo_s[pl.ds(dest[p], 1), :], hi_s[pl.ds(dest[p], 1), :]
            )
            if p == 7:
                c_buf[7] = value
                meta_recv[7] = bounds
            else:
                send_buf[p] = value
                meta_send[p] = bounds
                c_copies[p].start()
                m_copies[p].start()

    for copy in h_copies:
        copy.wait()
    h = h_buf[...].reshape(8 * cap, ff)
    gl_s[...] = nt_dot(h, h)
    share = ff // (NX * nz)
    na = X_FIRST
    nb = share - na
    split = NX * nz * na
    j = iota((ff, 1), 0).astype(F32)
    qa = jnp.floor((j + 0.5) * (1.0 / na))
    unit_a = share * qa + (j - na * qa)
    jb = j - split
    qb = jnp.floor((jb + 0.5) * (1.0 / nb))
    zb = jnp.floor((qb + 0.5) * (1.0 / NX))
    unit_b = share * (nz * (qb - NX * zb) + zb) + na + (jb - nb * qb)
    unit = jnp.where(j < split, unit_a, unit_b)
    order = (iota((ff, ff), 1).astype(F32) == unit).astype(F32).astype(BF16)
    ht_s[...] = nt_dot(order, h).astype(BF16)

    for n in range(2):
        c_copies[n].wait_recv()
        relays[n].start()
    for p in range(7):
        m_copies[p].wait_recv()
    slot_128 = iota((cap, 128), 0).astype(F32)
    member = jnp.concatenate(
        [
            jnp.where(
                (slot_128 >= meta_recv[p, 0:1, :]) & (slot_128 < meta_recv[p, 1:2, :]), 1.0, 0.0
            )
            for p in range(8)
        ],
        axis=0,
    )
    member_b = member.astype(BF16)
    gl_s[...] = gl_s[...] * nt_dot(member_b, member_b)
    for p in range(2, 7):
        c_copies[p].wait_recv()
    for copy in relays:
        copy.wait_recv()
    cot = c_buf[...].reshape(8 * cap, dw)
    spread = jnp.sum(gl_s[...] * nt_dot(cot, cot), axis=1, keepdims=True)
    squares = jnp.sum(member * spread, axis=0, keepdims=True)
    sq_send[...] = jnp.broadcast_to(squares, (8, 128))
    q_copies = [link(sq_send, sq_recv.at[p], expert_at(*REL[p])) for p in range(7)]
    for copy in q_copies:
        copy.start()
    total = squares
    for p in range(7):
        q_copies[p].wait_recv()
        total = total + sq_recv[p, 0:1, :]
    clip = 1.0 / jnp.maximum(jnp.sqrt(total / (ff * dw)), 1.0)
    slot_weight = jnp.sum(member * clip, axis=1, keepdims=True) / EXAMPLES
    scaled_s[...] = (slot_weight * cot.astype(F32)).astype(BF16)

    ra, rb = na * lanes, nb * lanes
    rows_a = nz * na
    half = nz // 2

    def gradient_a(chunk):
        value = nn_dot(ht_s[pl.ds(pl.multiple_of(chunk * rows_a, 16), rows_a), :], scaled_s[...])
        for n in range(lanes):
            acc_a[chunk, pl.ds(n, rows_a, stride=lanes), :] = value[:, n * 128 : (n + 1) * 128]

    def coded(value, count, rows):
        code, step = encode(value)
        return code.reshape(count, rows, 128).astype(jnp.int16), step

    lower, upper = pl.ds(0, half * ra), pl.ds(half * ra, half * ra)

    def x_message(n, place):
        return [
            link(x_codes.at[n], x_in.at[n], place), link(x_steps.at[n], x_in_steps.at[n], place)
        ]

    def x_send(n, value, message):
        x_codes[n], x_steps[n] = coded(value, half, ra)
        for copy in message:
            copy.start()

    def x_value(n):
        return decode(x_in[n], x_in_steps[n, 0:1, :]).reshape(half * ra, 128)

    messages = [x_message(n, x_at(1 if n % 2 == 0 else 3)) for n in range(6)]
    gradient_a(x2)
    x_send(0, acc_a[x2, lower, :], messages[0])
    x_send(1, acc_a[x2, upper, :], messages[1])
    gradient_a(xp)
    x_send(2, acc_a[xp, upper, :], messages[2])
    gradient_a(xm)
    x_send(3, acc_a[xm, lower, :], messages[3])

    value = nn_dot(ht_s[split:, :], scaled_s[...])
    for n in range(lanes):
        acc_b[pl.ds(n, NX * nz * nb, stride=lanes), :] = value[:, n * 128 : (n + 1) * 128]

    def z_start(which, sums, rows, codes, taken, side):
        codes[...], z_steps[which] = coded(sums, nz, rows)
        started = []
        near = ((2, 0), (-2, 1), (1, 2), (-1, 3))
        plan = [(o, n, ((0, 0), (5, 1), (-5, 2))) for o, n in near]
        plan.insert(2, (3 * side, 4, ((5 * side, 0),)))
        for o, n, wanted in plan:
            started.append(link(z_steps.at[which], z_in_steps.at[which, n], z_at(o)))
            for d, m in wanted:
                started.append(
                    link(codes.at[(z + nz + o + d) % nz], taken.at[3 * n + m], z_at(o))
                )
        for copy in started:
            copy.start()
        return started

    def z_middle(which, started, sums_at, rows, taken, codes, taken2, side):
        for copy in started:
            copy.wait_recv()
        pieces = [sums_at(z), sums_at((z + 5) % nz), sums_at((z + nz - 5) % nz)]
        for n in range(4):
            for m in range(3):
                pieces[m] = pieces[m] + decode(taken[3 * n + m], z_in_steps[which, n, 0:1, :])
        far = 1 if side == 1 else 2
        pieces[far] = pieces[far] + decode(taken[12], z_in_steps[which, 4, 0:1, :])
        codes[...], z_steps[2 + which] = coded(jnp.concatenate(pieces[1:], axis=0), 2, rows)
        started = []
        for n, o in enumerate((5, -5)):
            started.append(link(z_steps.at[2 + which], z_in_steps.at[which, 5 + n], z_at(o)))
            started.append(link(codes.at[n], taken2.at[n], z_at(o)))
        for copy in started:
            copy.start()
        return pieces[0], started

    def z_end(which, value, started, taken2):
        for copy in started:
            copy.wait_recv()
        for n in range(2):
            value = value + decode(taken2[n], z_in_steps[which, 5 + n, 0:1, :])
        return value

    def a_at(d):
        return acc_a[x, pl.ds(pl.multiple_of(d * ra, 8), ra), :]

    def b_at(d):
        return acc_b[pl.ds(pl.multiple_of(d * NX * rb, 8), NX * rb), :]

    b_started = z_start(1, acc_b[...], NX * rb, zb_codes, zb_in, -1)
    gradient_a(x)
    for n, chunk, part in ((4, xp, lower), (5, xm, upper)):
        for copy in messages[n - 4]:
            copy.wait_recv()
        x_send(n, acc_a[chunk, part, :] + x_value(n - 4), messages[n])
    for n in (2, 3, 4, 5):
        for copy in messages[n]:
            copy.wait_recv()
    acc_a[x, lower, :] = acc_a[x, lower, :] + (x_value(4) + x_value(3))
    acc_a[x, upper, :] = acc_a[x, upper, :] + (x_value(2) + x_value(5))
    a_started = z_start(0, acc_a[x], ra, za_codes, za_in, 1)
    b_sum, b_started = z_middle(1, b_started, b_at, NX * rb, zb_in, zb2_codes, zb2_in, -1)
    a_sum, a_started = z_middle(0, a_started, a_at, ra, za_in, za2_codes, za2_in, 1)
    b_sum = z_end(1, b_sum, b_started, zb2_in)
    bx_codes[...], bx_steps[0] = coded(b_sum, NX, rb)
    acc_b[pl.ds(0, NX * rb), :] = b_sum
    last = []
    for n, dx in enumerate((2, 1, 3)):
        last.append(link(bx_steps.at[0], bx_steps.at[1 + n], x_at(dx)))
        last.append(link(bx_codes.at[(x + dx) % NX], bx_in.at[n], x_at(dx)))
    for copy in last:
        copy.start()
    out_ref[0:ra, :] = z_end(0, a_sum, a_started, za2_in)
    value = acc_b[pl.ds(pl.multiple_of(x * rb, 8), rb), :]
    for copy in last:
        copy.wait_recv()
    for n in range(3):
        value = value + decode(bx_in[n], bx_steps[1 + n, 0:1, :])
    out_ref[ra:, :] = value
    for copy in copies:
        copy.wait_send()


def shards(nz, grad_out, routes, route_weight, example_ids, example_weight, hidden):
    tok, dw = grad_out.shape
    cap, ff = hidden.shape[3:]
    lanes = dw // 128
    share = ff // (NX * nz)
    ra, rb = X_FIRST * lanes, (share - X_FIRST) * lanes
    half = nz // 2
    i16 = jnp.int16
    dma = pltpu.SemaphoreType.DMA
    scratch = [
        pltpu.VMEM((tok, dw), BF16),
        pltpu.VMEM((TOP, tok), jnp.int32),
        pltpu.VMEM((TOP, tok), F32),
        pltpu.VMEM((1, tok), jnp.int32),
        pltpu.VMEM((1, EXAMPLES), F32),
        pltpu.VMEM((8, cap, ff), BF16),
        pltpu.VMEM((8, tok), F32),
        pltpu.VMEM((8, tok), F32),
        pltpu.VMEM((8, 128), F32),
        pltpu.VMEM((8, 128), F32),
        pltpu.VMEM((7, cap, dw), BF16),
        pltpu.VMEM((2, cap, dw), BF16),
        pltpu.VMEM((8, cap, dw), BF16),
        pltpu.VMEM((7, 8, 128), F32),
        pltpu.VMEM((8, 8, 128), F32),
        pltpu.VMEM((8, 128), F32),
        pltpu.VMEM((7, 8, 128), F32),
        pltpu.VMEM((8 * cap, 8 * cap), F32),
        pltpu.VMEM((ff, 8 * cap), BF16),
        pltpu.VMEM((8 * cap, dw), BF16),
        pltpu.VMEM((NX, nz * ra, 128), F32),
        pltpu.VMEM((nz * NX * rb, 128), F32),
        pltpu.VMEM((6, half, ra, 128), i16),
        pltpu.VMEM((6, 8, 128), F32),
        pltpu.VMEM((6, half, ra, 128), i16),
        pltpu.VMEM((6, 8, 128), F32),
        pltpu.VMEM((nz, ra, 128), i16),
        pltpu.VMEM((13, ra, 128), i16),
        pltpu.VMEM((nz, NX * rb, 128), i16),
        pltpu.VMEM((13, NX * rb, 128), i16),
        pltpu.VMEM((2, ra, 128), i16),
        pltpu.VMEM((2, ra, 128), i16),
        pltpu.VMEM((2, NX * rb, 128), i16),
        pltpu.VMEM((2, NX * rb, 128), i16),
        pltpu.VMEM((4, 8, 128), F32),
        pltpu.VMEM((2, 7, 8, 128), F32),
        pltpu.VMEM((NX, rb, 128), i16),
        pltpu.VMEM((3, rb, 128), i16),
        pltpu.VMEM((4, 8, 128), F32),
        dma((13,)), dma((LINKS,)), dma((LINKS,)),
    ]
    out = pl.pallas_call(
        functools.partial(body, (nz, ff, dw, cap, tok)),
        out_shape=jax.ShapeDtypeStruct((share * lanes, 128), F32),
        in_specs=[pl.BlockSpec(memory_space=pl.ANY)] * 6,
        out_specs=pl.BlockSpec(memory_space=pltpu.VMEM),
        scratch_shapes=scratch,
        compiler_params=pltpu.CompilerParams(
            collective_id=0, has_side_effects=True, vmem_limit_bytes=62 * 1024 * 1024
        ),
        name="clipped_grads",
    )(grad_out, routes.T, route_weight.T, example_ids, example_weight, hidden[0, 0])
    return out.reshape(share, 1, dw)


def solution(mesh):
    nz = mesh.shape["dp"] // NX
    placed = (
        P(("dp", "expert"), None),
        P(("dp", "expert"), None),
        P(("dp", "expert"), None),
        P("dp", "expert"),
        P("dp", None),
        P("dp", "expert", None, None, None),
    )
    return jax.shard_map(
        functools.partial(shards, nz), mesh=mesh, in_specs=placed,
        out_specs=P("dp", "expert", None), check_vma=False,
    )
```

```python
import functools

import jax
import jax.numpy as jnp
from jax import lax
from jax.experimental import pallas as pl
from jax.experimental.pallas import tpu as pltpu
from jax.sharding import PartitionSpec as P

EXAMPLES = 8
TOP = 6
NX = 4
MESH = pl.DeviceIdType.MESH
F32 = jnp.float32
BF16 = jnp.bfloat16

RUNS = (4, 3)
LINKS = 128

REL = ((2, 0), (2, 1), (1, 0), (3, 0), (1, 1), (3, 1), (0, 1), (0, 0))


def nt_dot(a, b):
    return lax.dot_general(a, b, (((1,), (1,)), ((), ())), preferred_element_type=F32)


def nn_dot(a, b):
    return lax.dot_general(a, b, (((1,), (0,)), ((), ())), preferred_element_type=F32)


def iota(shape, dim):
    return lax.broadcasted_iota(jnp.int32, shape, dim)


def other(src, dst, send_sem, recv_sem, **device):
    return pltpu.make_async_remote_copy(
        src_ref=src, dst_ref=dst, send_sem=send_sem, recv_sem=recv_sem,
        device_id=device, device_id_type=MESH,
    )


def encode(value):
    most = jnp.max(jnp.abs(value), axis=0, keepdims=True)
    step = jnp.maximum(most, 1e-33) * (1.0 / 32760.0)
    code = jnp.round(value * (1.0 / step)).astype(jnp.int32)
    return code, step


def decode(code, step):
    return code.astype(jnp.int32).astype(F32) * step


def body(
    cfg,
    go_hbm, routes_hbm, weight_hbm, ids_hbm, ew_hbm, h_ref,
    out_ref,
    go_ref, routes_ref, weight_ref, ids_ref, ew_ref,
    h_buf, rank_s, scale_s, lo_s, hi_s, send_buf, relay_buf, c_buf, meta_send, meta_recv, sq_send, sq_recv,
    gl_s, ht_s, scaled_s, parts,
    local_sem, send_sem, recv_sem,
):
    nz, ff, dw, cap, tok = cfg
    lanes = dw // 128
    dp, me = lax.axis_index("dp"), lax.axis_index("expert")
    x, z = dp // nz, dp % nz
    y, core = me // 2, me % 2
    xp, xm, x2 = (x + 1) % NX, (x + 3) % NX, (x + 2) % NX

    def expert_at(dy, dc):
        return dict(expert=((y + dy) % 4) * 2 + (core + dc) % 2)

    def x_at(dx):
        return dict(dp=((x + dx) % NX) * nz + z)

    def z_at(dz):
        return dict(dp=x * nz + (z + nz + dz) % nz)

    dest = [expert_at(dy, dc)["expert"] for dy, dc in REL]
    source = [((y + 4 - dy) % 4) * 2 + (core + 2 - dc) % 2 for dy, dc in REL]
    copies = []

    def link(src, dst, place):
        n = len(copies)
        copies.append(other(src, dst, send_sem.at[n], recv_sem.at[n], **place))
        return copies[-1]

    barrier = pltpu.get_barrier_semaphore()
    greeted = [expert_at(dy, dc) for dy, dc in REL[:7]]
    greeted += [x_at(dx) for dx in (1, 2, 3)] + [z_at(dz) for dz in (1, -1, 2, -2, 3, -3)]
    for place in greeted:
        pl.semaphore_signal(barrier, inc=1, device_id=place, device_id_type=MESH)

    inputs = [
        pltpu.make_async_copy(src, dst, local_sem.at[n])
        for n, (src, dst) in enumerate((
            (routes_hbm, routes_ref), (weight_hbm, weight_ref), (ids_hbm, ids_ref),
            (ew_hbm, ew_ref), (go_hbm, go_ref),
        ))
    ]
    for copy in inputs:
        copy.start()
    h_copies = [
        pltpu.make_async_copy(h_ref.at[source[p]], h_buf.at[p], local_sem.at[5 + p])
        for p in range(8)
    ]
    for copy in h_copies:
        copy.start()
    for copy in inputs[:4]:
        copy.wait()

    expert_row = iota((8, tok), 0)
    routed = jnp.zeros((8, tok), F32)
    weight = jnp.zeros((8, tok), F32)
    for k in range(TOP):
        match = routes_ref[k : k + 1, :] == expert_row
        routed = jnp.where(match, 1.0, routed)
        weight = jnp.where(match, weight_ref[k : k + 1, :], weight)
    ids = ids_ref[...]
    token_weight = jnp.zeros((1, tok), F32)
    for example in range(EXAMPLES):
        token_weight = jnp.where(
            ids == example, ew_ref[0:1, example : example + 1], token_weight
        )
    earlier = (iota((tok, tok), 0) < iota((tok, tok), 1)).astype(F32).astype(BF16)
    routed_b = routed.astype(BF16)
    rank = nn_dot(routed_b, earlier)
    rank_s[...] = jnp.where(routed > 0.5, rank, -1.0)
    scale_s[...] = weight * token_weight
    example_col = iota((128, tok), 0)
    lo_s[...] = nt_dot(routed_b, (ids < example_col).astype(F32).astype(BF16))
    hi_s[...] = nt_dot(routed_b, (ids <= example_col).astype(F32).astype(BF16))

    slot_col = iota((cap, tok), 0).astype(F32)
    sub2 = iota((2, 128), 0)
    c_copies = [
        link(send_buf.at[0], relay_buf.at[0], expert_at(1, 0)),
        link(send_buf.at[1], relay_buf.at[1], expert_at(3, 0)),
    ]
    c_copies += [link(send_buf.at[p], c_buf.at[p], expert_at(*REL[p])) for p in range(2, 7)]
    relays = [
        link(relay_buf.at[0], c_buf.at[0], expert_at(1, 0)),
        link(relay_buf.at[1], c_buf.at[1], expert_at(3, 1)),
    ]
    m_copies = [link(meta_send.at[p], meta_recv.at[p], expert_at(*REL[p])) for p in range(7)]
    inputs[4].wait()
    for batch in ((0, 1), (2, 3, 4, 5), (6, 7)):
        masks, scales = [], []
        for p in batch:
            hit = rank_s[pl.ds(dest[p], 1), :] == slot_col
            masks.append(hit.astype(F32).astype(BF16))
            scales.append(
                jnp.sum(jnp.where(hit, scale_s[pl.ds(dest[p], 1), :], 0.0), axis=1, keepdims=True)
            )
        rows = nn_dot(jnp.concatenate(masks, axis=0), go_ref[...])
        if batch[0] == 0:
            pl.semaphore_wait(barrier, len(greeted))
        for i, p in enumerate(batch):
            value = (rows[i * cap : (i + 1) * cap, :] * scales[i]).astype(BF16)
            bounds = jnp.where(
                sub2 == 0, lo_s[pl.ds(dest[p], 1), :], hi_s[pl.ds(dest[p], 1), :]
            )
            if p == 7:
                c_buf[7] = value
                meta_recv[7] = bounds
            else:
                send_buf[p] = value
                meta_send[p] = bounds
                c_copies[p].start()
                m_copies[p].start()

    for copy in h_copies:
        copy.wait()
    h = h_buf[...].reshape(8 * cap, ff)
    gl_s[...] = nt_dot(h, h)
    share = ff // (NX * nz)
    j = iota((ff, 1), 0).astype(F32)
    unit, start, taken = j, 0, 0
    starts = []
    for n, rows in enumerate(RUNS + (share - sum(RUNS),)):
        at = j - start
        q = jnp.floor((at + 0.5) * (1.0 / rows))
        r = at - rows * q
        if n == len(RUNS):
            zq = jnp.floor((q + 0.5) * (1.0 / NX))
            q = nz * (q - NX * zq) + zq
        unit = jnp.where(j >= start, share * q + taken + r, unit)
        starts.append(start)
        start, taken = start + NX * nz * rows, taken + rows
    order = (iota((ff, ff), 1).astype(F32) == unit).astype(F32).astype(BF16)
    ht_s[...] = nt_dot(order, h).astype(BF16)

    for n in range(2):
        c_copies[n].wait_recv()
        relays[n].start()
    for p in range(7):
        m_copies[p].wait_recv()
    slot_128 = iota((cap, 128), 0).astype(F32)
    member = jnp.concatenate(
        [
            jnp.where(
                (slot_128 >= meta_recv[p, 0:1, :]) & (slot_128 < meta_recv[p, 1:2, :]), 1.0, 0.0
            )
            for p in range(8)
        ],
        axis=0,
    )
    member_b = member.astype(BF16)
    gl_s[...] = gl_s[...] * nt_dot(member_b, member_b)
    for p in range(2, 7):
        c_copies[p].wait_recv()
    for copy in relays:
        copy.wait_recv()
    cot = c_buf[...].reshape(8 * cap, dw)
    spread = jnp.sum(gl_s[...] * nt_dot(cot, cot), axis=1, keepdims=True)
    squares = jnp.sum(member * spread, axis=0, keepdims=True)
    sq_send[...] = squares
    q_copies = [link(sq_send, sq_recv.at[p], expert_at(*REL[p])) for p in range(7)]
    for copy in q_copies:
        copy.start()
    total = squares
    for p in range(7):
        q_copies[p].wait_recv()
        total = total + sq_recv[p]
    clip = 1.0 / jnp.maximum(jnp.sqrt(total / (ff * dw)), 1.0)
    slot_weight = jnp.sum(member * clip, axis=1, keepdims=True) / EXAMPLES
    scaled_s[...] = (slot_weight * cot.astype(F32)).astype(BF16)

    half = nz // 2

    def begin(messages):
        for copy in messages:
            copy.start()

    def arrive(messages):
        for copy in messages:
            copy.wait_recv()

    def gradient(dst, start, rows):
        value = nn_dot(ht_s[pl.ds(start, rows), :], scaled_s[...])
        for n in range(lanes):
            dst[pl.ds(n, rows, stride=lanes), :] = value[:, n * 128 : (n + 1) * 128]

    class AlongX:
        def __init__(self, n):
            self.start, self.rows = starts[n], nz * RUNS[n]
            self.chunk = RUNS[n] * lanes
            self.half = half * self.chunk
            self.lower, self.upper = pl.ds(0, self.half), pl.ds(self.half, self.half)
            refs = parts[n]
            self.sums, self.z = refs["sums"], refs["z"]
            self.codes, self.steps = refs["x_codes"], refs["x_steps"]
            self.taken, self.taken_steps = refs["x_in"], refs["x_in_steps"]
            self.messages = []
            for m in range(6):
                place = x_at(1 if m % 2 == 0 else 3)
                self.messages.append([
                    link(self.steps.at[m], self.taken_steps.at[m], place),
                    link(self.codes.at[m], self.taken.at[m], place),
                ])

        def gradient(self, quarter):
            start = pl.multiple_of(self.start + quarter * self.rows, 16)
            gradient(self.sums.at[quarter], start, self.rows)

        def send(self, m, value):
            code, self.steps[m] = encode(value)
            self.codes[m] = code.astype(jnp.int16)
            begin(self.messages[m])

        def value(self, m):
            return decode(self.taken[m], self.taken_steps[m])

        def opposite(self):
            self.gradient(x2)
            self.send(0, self.sums[x2, self.lower, :])
            self.send(1, self.sums[x2, self.upper, :])

        def near(self):
            self.gradient(xp)
            self.send(2, self.sums[xp, self.upper, :])
            self.gradient(xm)
            self.send(3, self.sums[xm, self.lower, :])

        def relay(self):
            arrive(self.messages[0])
            self.send(4, self.sums[xp, self.lower, :] + self.value(0))
            arrive(self.messages[1])
            self.send(5, self.sums[xm, self.upper, :] + self.value(1))

        def finish(self):
            for m in (2, 3, 4, 5):
                arrive(self.messages[m])
            self.sums[x, self.lower, :] = self.sums[x, self.lower, :] + (self.value(4) + self.value(3))
            self.sums[x, self.upper, :] = self.sums[x, self.upper, :] + (self.value(2) + self.value(5))

        def at(self, d):
            return self.sums[x, pl.ds(pl.multiple_of(d * self.chunk, 8), self.chunk), :]

    def z_start(refs, sums, rows, side):
        code, refs["steps"][0] = encode(sums)
        refs["codes"][...] = code.reshape(nz, rows, 128).astype(jnp.int16)
        plan = [(o, n, ((0, 0), (5, 1), (-5, 2))) for o, n in ((2, 0), (-2, 1), (1, 2), (-1, 3))]
        plan.insert(2, (3 * side, 4, ((5 * side, 0),)))
        started = []
        for o, n, wanted in plan:
            started.append(link(refs["steps"].at[0], refs["in_steps"].at[n], z_at(o)))
            for d, m in wanted:
                started.append(
                    link(refs["codes"].at[(z + nz + o + d) % nz], refs["in"].at[3 * n + m], z_at(o))
                )
        begin(started)
        return started

    def z_middle(refs, started, sums_at, side):
        arrive(started)
        pieces = [sums_at(z), sums_at((z + 5) % nz), sums_at((z + nz - 5) % nz)]
        for n in range(4):
            for m in range(3):
                pieces[m] = pieces[m] + decode(refs["in"][3 * n + m], refs["in_steps"][n])
        far = 1 if side == 1 else 2
        pieces[far] = pieces[far] + decode(refs["in"][12], refs["in_steps"][4])
        return pieces

    def z_second(refs, pieces, rows):
        code, refs["steps"][1] = encode(jnp.concatenate(pieces[1:], axis=0))
        refs["codes2"][...] = code.reshape(2, rows, 128).astype(jnp.int16)
        refs["own"][...] = pieces[0]
        started = []
        for n, o in enumerate((5, -5)):
            started.append(link(refs["steps"].at[1], refs["in_steps"].at[5 + n], z_at(o)))
            started.append(link(refs["codes2"].at[n], refs["in2"].at[n], z_at(o)))
        begin(started)
        return started

    def z_end(refs, started):
        arrive(started)
        value = refs["own"][...]
        for n in range(2):
            value = value + decode(refs["in2"][n], refs["in_steps"][5 + n])
        return value

    refs_b = parts[-1]
    zb = refs_b["z"]
    rb = (share - sum(RUNS)) * lanes
    sums_b = refs_b["sums"]

    def b_at(d):
        return sums_b[pl.ds(pl.multiple_of(d * NX * rb, 8), NX * rb), :]

    one, two = AlongX(0), AlongX(1)
    one.opposite()
    gradient(sums_b, starts[-1], NX * nz * (rb // lanes))
    started_b = z_start(zb, sums_b[...], NX * rb, -1)
    one.near()
    two.opposite()
    one.relay()
    two.near()
    one.gradient(x)
    two.gradient(x)
    two.relay()
    one.finish()
    started_1 = z_start(one.z, one.sums[x], one.chunk, 1)
    two.finish()
    started_2 = z_start(two.z, two.sums[x], two.chunk, 1)

    pieces = z_middle(zb, started_b, b_at, -1)
    value = jnp.concatenate([p.reshape(NX, rb, 128) for p in pieces], axis=1)
    refs_b["x_own"][...] = value
    code, refs_b["x_steps"][0] = encode(value.reshape(NX * 3 * rb, 128))
    refs_b["x_codes"][...] = code.reshape(NX, 3 * rb, 128).astype(jnp.int16)
    across = []
    for n, dx in enumerate((2, 1, 3)):
        across.append(link(refs_b["x_steps"].at[0], refs_b["x_steps"].at[1 + n], x_at(dx)))
        across.append(link(refs_b["x_codes"].at[(x + dx) % NX], refs_b["x_in"].at[n], x_at(dx)))
    begin(across)

    pieces = z_middle(one.z, started_1, one.at, 1)
    started_1 = z_second(one.z, pieces, one.chunk)
    pieces = z_middle(two.z, started_2, two.at, 1)
    started_2 = z_second(two.z, pieces, two.chunk)
    arrive(across)
    value = refs_b["x_own"][x]
    for n in range(3):
        value = value + decode(refs_b["x_in"][n], refs_b["x_steps"][1 + n])
    started_b = z_second(zb, [value[n * rb : (n + 1) * rb, :] for n in range(3)], rb)
    out_ref[0 : one.chunk, :] = z_end(one.z, started_1)
    out_ref[one.chunk : one.chunk + two.chunk, :] = z_end(two.z, started_2)
    out_ref[one.chunk + two.chunk :, :] = z_end(zb, started_b)
    for copy in copies:
        copy.wait_send()


def shards(nz, grad_out, routes, route_weight, example_ids, example_weight, hidden):
    tok, dw = grad_out.shape
    cap, ff = hidden.shape[3:]
    lanes = dw // 128
    share = ff // (NX * nz)
    half = nz // 2
    i16 = jnp.int16

    def z_refs(rows, last):
        return dict(
            codes=pltpu.VMEM((nz, rows, 128), i16),
            steps=pltpu.VMEM((2, 1, 128), F32),
            **{"in": pltpu.VMEM((13, rows, 128), i16)},
            in_steps=pltpu.VMEM((7, 1, 128), F32),
            codes2=pltpu.VMEM((2, last, 128), i16),
            in2=pltpu.VMEM((2, last, 128), i16),
            own=pltpu.VMEM((last, 128), F32),
        )

    parts = []
    for rows in RUNS:
        chunk = rows * lanes
        parts.append(dict(
            sums=pltpu.VMEM((NX, nz * chunk, 128), F32),
            x_codes=pltpu.VMEM((6, half * chunk, 128), i16),
            x_steps=pltpu.VMEM((6, 1, 128), F32),
            x_in=pltpu.VMEM((6, half * chunk, 128), i16),
            x_in_steps=pltpu.VMEM((6, 1, 128), F32),
            z=z_refs(chunk, chunk),
        ))
    rb = (share - sum(RUNS)) * lanes
    parts.append(dict(
        sums=pltpu.VMEM((nz * NX * rb, 128), F32),
        x_own=pltpu.VMEM((NX, 3 * rb, 128), F32),
        x_codes=pltpu.VMEM((NX, 3 * rb, 128), i16),
        x_in=pltpu.VMEM((3, 3 * rb, 128), i16),
        x_steps=pltpu.VMEM((4, 1, 128), F32),
        z=z_refs(NX * rb, rb),
    ))
    dma = pltpu.SemaphoreType.DMA
    scratch = [
        pltpu.VMEM((tok, dw), BF16),
        pltpu.VMEM((TOP, tok), jnp.int32),
        pltpu.VMEM((TOP, tok), F32),
        pltpu.VMEM((1, tok), jnp.int32),
        pltpu.VMEM((1, EXAMPLES), F32),
        pltpu.VMEM((8, cap, ff), BF16),
        pltpu.VMEM((8, tok), F32),
        pltpu.VMEM((8, tok), F32),
        pltpu.VMEM((8, 128), F32),
        pltpu.VMEM((8, 128), F32),
        pltpu.VMEM((7, cap, dw), BF16),
        pltpu.VMEM((2, cap, dw), BF16),
        pltpu.VMEM((8, cap, dw), BF16),
        pltpu.VMEM((7, 2, 128), F32),
        pltpu.VMEM((8, 2, 128), F32),
        pltpu.VMEM((1, 128), F32),
        pltpu.VMEM((7, 1, 128), F32),
        pltpu.VMEM((8 * cap, 8 * cap), F32),
        pltpu.VMEM((ff, 8 * cap), BF16),
        pltpu.VMEM((8 * cap, dw), BF16),
        parts,
        dma((13,)), dma((LINKS,)), dma((LINKS,)),
    ]
    out = pl.pallas_call(
        functools.partial(body, (nz, ff, dw, cap, tok)),
        out_shape=jax.ShapeDtypeStruct((share * lanes, 128), F32),
        in_specs=[pl.BlockSpec(memory_space=pl.ANY)] * 6,
        out_specs=pl.BlockSpec(memory_space=pltpu.VMEM),
        scratch_shapes=scratch,
        compiler_params=pltpu.CompilerParams(
            collective_id=0, has_side_effects=True, vmem_limit_bytes=62 * 1024 * 1024
        ),
        name="clipped_grads",
    )(grad_out, routes.T, route_weight.T, example_ids, example_weight, hidden[0, 0])
    return out.reshape(share, 1, dw)


def solution(mesh):
    nz = mesh.shape["dp"] // NX
    placed = (
        P(("dp", "expert"), None),
        P(("dp", "expert"), None),
        P(("dp", "expert"), None),
        P("dp", "expert"),
        P("dp", None),
        P("dp", "expert", None, None, None),
    )
    return jax.shard_map(
        functools.partial(shards, nz), mesh=mesh, in_specs=placed,
        out_specs=P("dp", "expert", None), check_vma=False,
    )
```

```python
import functools

import jax
import jax.numpy as jnp
from jax import lax
from jax.experimental import pallas as pl
from jax.experimental.pallas import tpu as pltpu
from jax.sharding import PartitionSpec as P

EXAMPLES = 8
TOP = 6
NX = 4
MESH = pl.DeviceIdType.MESH
F32 = jnp.float32
BF16 = jnp.bfloat16

RUNS = (4, 4)
LINKS = 112
STRIDE = 5

REL = ((2, 0), (2, 1), (1, 0), (3, 0), (1, 1), (3, 1), (0, 1), (0, 0))


def nt_dot(a, b):
    return lax.dot_general(a, b, (((1,), (1,)), ((), ())), preferred_element_type=F32)


def nn_dot(a, b):
    return lax.dot_general(a, b, (((1,), (0,)), ((), ())), preferred_element_type=F32)


def iota(shape, dim):
    return lax.broadcasted_iota(jnp.int32, shape, dim)


def other(src, dst, send_sem, recv_sem, **device):
    return pltpu.make_async_remote_copy(
        src_ref=src, dst_ref=dst, send_sem=send_sem, recv_sem=recv_sem,
        device_id=device, device_id_type=MESH,
    )


def encode(value):
    most = jnp.max(jnp.abs(value), axis=0, keepdims=True)
    step = jnp.maximum(most, 1e-33) * (1.0 / 32760.0)
    code = jnp.round(value * (1.0 / step)).astype(jnp.int32)
    return code, step


def decode(code, step):
    return code.astype(jnp.int32).astype(F32) * step


def body(
    cfg,
    go_hbm, routes_hbm, weight_hbm, ids_hbm, ew_hbm, h_ref,
    out_ref,
    go_ref, routes_ref, weight_ref, ids_ref, ew_ref,
    h_buf, rank_s, scale_s, lo_s, hi_s, send_buf, relay_buf, c_buf, meta_send, meta_recv, sq_send, sq_recv,
    gl_s, ht_s, scaled_s, parts,
    local_sem, send_sem, recv_sem,
):
    nz, ff, dw, cap, tok = cfg
    lanes = dw // 128
    dp, me = lax.axis_index("dp"), lax.axis_index("expert")
    x, z = dp // nz, dp % nz
    y, core = me // 2, me % 2
    xp, xm, x2 = (x + 1) % NX, (x + 3) % NX, (x + 2) % NX

    def expert_at(dy, dc):
        return dict(expert=((y + dy) % 4) * 2 + (core + dc) % 2)

    def x_at(dx):
        return dict(dp=((x + dx) % NX) * nz + z)

    def z_at(dz):
        return dict(dp=x * nz + (z + nz + dz) % nz)

    dest = [expert_at(dy, dc)["expert"] for dy, dc in REL]
    source = [((y + 4 - dy) % 4) * 2 + (core + 2 - dc) % 2 for dy, dc in REL]
    copies = []

    def link(src, dst, place):
        n = len(copies)
        copies.append(other(src, dst, send_sem.at[n], recv_sem.at[n], **place))
        return copies[-1]

    barrier = pltpu.get_barrier_semaphore()
    greeted = [expert_at(dy, dc) for dy, dc in REL[:7]]
    greeted += [x_at(dx) for dx in (1, 2, 3)] + [z_at(dz) for dz in (1, -1, 2, -2, 3, -3)]
    for place in greeted:
        pl.semaphore_signal(barrier, inc=1, device_id=place, device_id_type=MESH)

    inputs = [
        pltpu.make_async_copy(src, dst, local_sem.at[n])
        for n, (src, dst) in enumerate((
            (routes_hbm, routes_ref), (weight_hbm, weight_ref), (ids_hbm, ids_ref),
            (ew_hbm, ew_ref), (go_hbm, go_ref),
        ))
    ]
    for copy in inputs:
        copy.start()
    h_copies = [
        pltpu.make_async_copy(h_ref.at[source[p]], h_buf.at[p], local_sem.at[5 + p])
        for p in range(8)
    ]
    for copy in h_copies:
        copy.start()
    for copy in inputs[:4]:
        copy.wait()

    expert_row = iota((8, tok), 0)
    routed = jnp.zeros((8, tok), F32)
    weight = jnp.zeros((8, tok), F32)
    for k in range(TOP):
        match = routes_ref[k : k + 1, :] == expert_row
        routed = jnp.where(match, 1.0, routed)
        weight = jnp.where(match, weight_ref[k : k + 1, :], weight)
    ids = ids_ref[...]
    token_weight = jnp.zeros((1, tok), F32)
    for example in range(EXAMPLES):
        token_weight = jnp.where(
            ids == example, ew_ref[0:1, example : example + 1], token_weight
        )
    earlier = (iota((tok, tok), 0) < iota((tok, tok), 1)).astype(F32).astype(BF16)
    routed_b = routed.astype(BF16)
    rank = nn_dot(routed_b, earlier)
    rank_s[...] = jnp.where(routed > 0.5, rank, -1.0)
    scale_s[...] = weight * token_weight
    example_col = iota((128, tok), 0)
    lo_s[...] = nt_dot(routed_b, (ids < example_col).astype(F32).astype(BF16))
    hi_s[...] = nt_dot(routed_b, (ids <= example_col).astype(F32).astype(BF16))

    slot_col = iota((cap, tok), 0).astype(F32)
    sub2 = iota((2, 128), 0)
    c_copies = [
        link(send_buf.at[0], relay_buf.at[0], expert_at(1, 0)),
        link(send_buf.at[1], relay_buf.at[1], expert_at(3, 0)),
    ]
    c_copies += [link(send_buf.at[p], c_buf.at[p], expert_at(*REL[p])) for p in range(2, 7)]
    relays = [
        link(relay_buf.at[0], c_buf.at[0], expert_at(1, 0)),
        link(relay_buf.at[1], c_buf.at[1], expert_at(3, 1)),
    ]
    m_copies = [link(meta_send.at[p], meta_recv.at[p], expert_at(*REL[p])) for p in range(7)]
    inputs[4].wait()
    for batch in ((0, 1), (2, 3, 4, 5), (6, 7)):
        masks, scales = [], []
        for p in batch:
            hit = rank_s[pl.ds(dest[p], 1), :] == slot_col
            masks.append(hit.astype(F32).astype(BF16))
            scales.append(
                jnp.sum(jnp.where(hit, scale_s[pl.ds(dest[p], 1), :], 0.0), axis=1, keepdims=True)
            )
        rows = nn_dot(jnp.concatenate(masks, axis=0), go_ref[...])
        if batch[0] == 0:
            pl.semaphore_wait(barrier, len(greeted))
        for i, p in enumerate(batch):
            value = (rows[i * cap : (i + 1) * cap, :] * scales[i]).astype(BF16)
            bounds = jnp.where(
                sub2 == 0, lo_s[pl.ds(dest[p], 1), :], hi_s[pl.ds(dest[p], 1), :]
            )
            if p == 7:
                c_buf[7] = value
                meta_recv[7] = bounds
            else:
                send_buf[p] = value
                meta_send[p] = bounds
                c_copies[p].start()
                m_copies[p].start()

    for copy in h_copies:
        copy.wait()
    h = h_buf[...].reshape(8 * cap, ff)
    gl_s[...] = nt_dot(h, h)
    share = ff // (NX * nz)
    j = iota((ff, 1), 0).astype(F32)
    unit, start, taken = j, 0, 0
    starts = []
    for n, rows in enumerate(RUNS + (share - sum(RUNS),)):
        at = j - start
        q = jnp.floor((at + 0.5) * (1.0 / rows))
        r = at - rows * q
        if n == len(RUNS):
            zq = jnp.floor((q + 0.5) * (1.0 / NX))
            xq = q - NX * zq
        else:
            xq = jnp.floor((q + 0.5) * (1.0 / nz))
            zq = q - nz * xq
        zq = STRIDE * zq
        q = nz * xq + zq - nz * jnp.floor((zq + 0.5) * (1.0 / nz))
        unit = jnp.where(j >= start, share * q + taken + r, unit)
        starts.append(start)
        start, taken = start + NX * nz * rows, taken + rows
    order = (iota((ff, ff), 1).astype(F32) == unit).astype(F32).astype(BF16)
    ht_s[...] = nt_dot(order, h).astype(BF16)

    for n in range(2):
        c_copies[n].wait_recv()
        relays[n].start()
    for p in range(7):
        m_copies[p].wait_recv()
    slot_128 = iota((cap, 128), 0).astype(F32)
    member = jnp.concatenate(
        [
            jnp.where(
                (slot_128 >= meta_recv[p, 0:1, :]) & (slot_128 < meta_recv[p, 1:2, :]), 1.0, 0.0
            )
            for p in range(8)
        ],
        axis=0,
    )
    member_b = member.astype(BF16)
    gl_s[...] = gl_s[...] * nt_dot(member_b, member_b)
    for p in range(2, 7):
        c_copies[p].wait_recv()
    for copy in relays:
        copy.wait_recv()
    cot = c_buf[...].reshape(8 * cap, dw)
    spread = jnp.sum(gl_s[...] * nt_dot(cot, cot), axis=1, keepdims=True)
    squares = jnp.sum(member * spread, axis=0, keepdims=True)
    sq_send[...] = squares
    q_copies = [link(sq_send, sq_recv.at[p], expert_at(*REL[p])) for p in range(7)]
    for copy in q_copies:
        copy.start()
    total = squares
    for p in range(7):
        q_copies[p].wait_recv()
        total = total + sq_recv[p]
    clip = 1.0 / jnp.maximum(jnp.sqrt(total / (ff * dw)), 1.0)
    slot_weight = jnp.sum(member * clip, axis=1, keepdims=True) / EXAMPLES
    scaled_s[...] = (slot_weight * cot.astype(F32)).astype(BF16)

    half = nz // 2

    def begin(messages):
        for copy in messages:
            copy.start()

    def arrive(messages):
        for copy in messages:
            copy.wait_recv()

    def gradient(dst, start, rows):
        value = nn_dot(ht_s[pl.ds(start, rows), :], scaled_s[...])
        for n in range(lanes):
            dst[pl.ds(n, rows, stride=lanes), :] = value[:, n * 128 : (n + 1) * 128]

    class AlongX:
        def __init__(self, n):
            self.start, self.rows = starts[n], nz * RUNS[n]
            self.chunk = RUNS[n] * lanes
            self.half = half * self.chunk
            self.lower, self.upper = pl.ds(0, self.half), pl.ds(self.half, self.half)
            refs = parts[n]
            self.sums, self.z = refs["sums"], refs["z"]
            self.codes, self.steps = refs["x_codes"], refs["x_steps"]
            self.taken, self.taken_steps = refs["x_in"], refs["x_in_steps"]
            self.messages = []
            for m in range(6):
                place = x_at(1 if m % 2 == 0 else 3)
                self.messages.append([
                    link(self.steps.at[m], self.taken_steps.at[m], place),
                    link(self.codes.at[m], self.taken.at[m], place),
                ])

        def gradient(self, quarter):
            start = pl.multiple_of(self.start + quarter * self.rows, 16)
            gradient(self.sums.at[quarter], start, self.rows)

        def send(self, m, value):
            code, self.steps[m] = encode(value)
            self.codes[m] = code.astype(jnp.int16)
            begin(self.messages[m])

        def value(self, m):
            return decode(self.taken[m], self.taken_steps[m])

        def opposite(self):
            self.gradient(x2)
            self.send(0, self.sums[x2, self.lower, :])
            self.send(1, self.sums[x2, self.upper, :])

        def near(self):
            self.gradient(xp)
            self.send(2, self.sums[xp, self.upper, :])
            self.gradient(xm)
            self.send(3, self.sums[xm, self.lower, :])

        def relay(self):
            arrive(self.messages[0])
            self.send(4, self.sums[xp, self.lower, :] + self.value(0))
            arrive(self.messages[1])
            self.send(5, self.sums[xm, self.upper, :] + self.value(1))

        def finish(self):
            for m in (2, 3, 4, 5):
                arrive(self.messages[m])
            self.sums[x, self.lower, :] = self.sums[x, self.lower, :] + (self.value(4) + self.value(3))
            self.sums[x, self.upper, :] = self.sums[x, self.upper, :] + (self.value(2) + self.value(5))

        def at(self, n):
            return self.sums[x, pl.ds(pl.multiple_of(n * self.chunk, 8), self.chunk), :]

    def place(d):
        return (pow(STRIDE, -1, nz) * (z + nz + d)) % nz

    def z_start(refs, sums, rows, side):
        code, refs["steps"][0] = encode(sums)
        code = code.reshape(nz, rows, 128).astype(jnp.int16)
        refs["codes"][1 : nz + 1] = code
        refs["codes"][0] = code[nz - 1]
        refs["codes"][nz + 1] = code[0]
        started = []
        for n, o in enumerate((2, -2, 3 * side, 1, -1)):
            started.append(link(refs["steps"].at[0], refs["in_steps"].at[n], z_at(o)))
            if n == 2:
                src, dst = refs["codes"].at[1 + place(half)], refs["in_far"]
            else:
                src, dst = refs["codes"].at[pl.ds(place(o), 3)], refs["in"].at[n - n // 3]
            started.append(link(src, dst, z_at(o)))
        begin(started)
        return started

    def z_middle(refs, started, sums_at, side):
        arrive(started)
        pieces = [sums_at((place(0) + nz + d) % nz) for d in (-1, 0, 1)]
        for n in range(4):
            for m in range(3):
                pieces[m] = pieces[m] + decode(refs["in"][n, m], refs["in_steps"][n + n // 2])
        pieces[1 + side] = pieces[1 + side] + decode(refs["in_far"][...], refs["in_steps"][2])
        return pieces[1], pieces[2], pieces[0]

    def z_second(refs, pieces, rows):
        code, refs["steps"][1] = encode(jnp.concatenate(pieces[1:], axis=0))
        refs["codes2"][...] = code.reshape(2, rows, 128).astype(jnp.int16)
        refs["own"][...] = pieces[0]
        started = []
        for n, o in enumerate((5, -5)):
            started.append(link(refs["steps"].at[1], refs["in_steps"].at[5 + n], z_at(o)))
            started.append(link(refs["codes2"].at[n], refs["in2"].at[n], z_at(o)))
        begin(started)
        return started

    def z_end(refs, started):
        arrive(started)
        value = refs["own"][...]
        for n in range(2):
            value = value + decode(refs["in2"][n], refs["in_steps"][5 + n])
        return value

    refs_b = parts[-1]
    zb = refs_b["z"]
    rb = (share - sum(RUNS)) * lanes
    sums_b = refs_b["sums"]

    def b_at(n):
        return sums_b[pl.ds(pl.multiple_of(n * NX * rb, 8), NX * rb), :]

    one, two = AlongX(0), AlongX(1)
    one.opposite()
    gradient(sums_b, starts[-1], NX * nz * (rb // lanes))
    started_b = z_start(zb, sums_b[...], NX * rb, -1)
    one.near()
    two.opposite()
    one.relay()
    two.near()
    one.gradient(x)
    two.gradient(x)
    two.relay()
    one.finish()
    started_1 = z_start(one.z, one.sums[x], one.chunk, 1)
    two.finish()
    started_2 = z_start(two.z, two.sums[x], two.chunk, 1)

    pieces = z_middle(zb, started_b, b_at, -1)
    value = jnp.concatenate([p.reshape(NX, rb, 128) for p in pieces], axis=1)
    refs_b["x_own"][...] = value
    code, refs_b["x_steps"][0] = encode(value.reshape(NX * 3 * rb, 128))
    refs_b["x_codes"][...] = code.reshape(NX, 3 * rb, 128).astype(jnp.int16)
    across = []
    for n, dx in enumerate((2, 1, 3)):
        across.append(link(refs_b["x_steps"].at[0], refs_b["x_steps"].at[1 + n], x_at(dx)))
        across.append(link(refs_b["x_codes"].at[(x + dx) % NX], refs_b["x_in"].at[n], x_at(dx)))
    begin(across)

    pieces = z_middle(one.z, started_1, one.at, 1)
    started_1 = z_second(one.z, pieces, one.chunk)
    pieces = z_middle(two.z, started_2, two.at, 1)
    started_2 = z_second(two.z, pieces, two.chunk)
    arrive(across)
    value = refs_b["x_own"][x]
    for n in range(3):
        value = value + decode(refs_b["x_in"][n], refs_b["x_steps"][1 + n])
    started_b = z_second(zb, [value[n * rb : (n + 1) * rb, :] for n in range(3)], rb)
    out_ref[0 : one.chunk, :] = z_end(one.z, started_1)
    out_ref[one.chunk : one.chunk + two.chunk, :] = z_end(two.z, started_2)
    out_ref[one.chunk + two.chunk :, :] = z_end(zb, started_b)
    for copy in copies:
        copy.wait_send()


def shards(nz, grad_out, routes, route_weight, example_ids, example_weight, hidden):
    tok, dw = grad_out.shape
    cap, ff = hidden.shape[3:]
    lanes = dw // 128
    share = ff // (NX * nz)
    half = nz // 2
    i16 = jnp.int16

    def z_refs(rows, last):
        return dict(
            codes=pltpu.VMEM((nz + 2, rows, 128), i16),
            steps=pltpu.VMEM((2, 1, 128), F32),
            **{"in": pltpu.VMEM((4, 3, rows, 128), i16)},
            in_far=pltpu.VMEM((rows, 128), i16),
            in_steps=pltpu.VMEM((7, 1, 128), F32),
            codes2=pltpu.VMEM((2, last, 128), i16),
            in2=pltpu.VMEM((2, last, 128), i16),
            own=pltpu.VMEM((last, 128), F32),
        )

    parts = []
    for rows in RUNS:
        chunk = rows * lanes
        parts.append(dict(
            sums=pltpu.VMEM((NX, nz * chunk, 128), F32),
            x_codes=pltpu.VMEM((6, half * chunk, 128), i16),
            x_steps=pltpu.VMEM((6, 1, 128), F32),
            x_in=pltpu.VMEM((6, half * chunk, 128), i16),
            x_in_steps=pltpu.VMEM((6, 1, 128), F32),
            z=z_refs(chunk, chunk),
        ))
    rb = (share - sum(RUNS)) * lanes
    parts.append(dict(
        sums=pltpu.VMEM((nz * NX * rb, 128), F32),
        x_own=pltpu.VMEM((NX, 3 * rb, 128), F32),
        x_codes=pltpu.VMEM((NX, 3 * rb, 128), i16),
        x_in=pltpu.VMEM((3, 3 * rb, 128), i16),
        x_steps=pltpu.VMEM((4, 1, 128), F32),
        z=z_refs(NX * rb, rb),
    ))
    dma = pltpu.SemaphoreType.DMA
    scratch = [
        pltpu.VMEM((tok, dw), BF16),
        pltpu.VMEM((TOP, tok), jnp.int32),
        pltpu.VMEM((TOP, tok), F32),
        pltpu.VMEM((1, tok), jnp.int32),
        pltpu.VMEM((1, EXAMPLES), F32),
        pltpu.VMEM((8, cap, ff), BF16),
        pltpu.VMEM((8, tok), F32),
        pltpu.VMEM((8, tok), F32),
        pltpu.VMEM((8, 128), F32),
        pltpu.VMEM((8, 128), F32),
        pltpu.VMEM((7, cap, dw), BF16),
        pltpu.VMEM((2, cap, dw), BF16),
        pltpu.VMEM((8, cap, dw), BF16),
        pltpu.VMEM((7, 2, 128), F32),
        pltpu.VMEM((8, 2, 128), F32),
        pltpu.VMEM((1, 128), F32),
        pltpu.VMEM((7, 1, 128), F32),
        pltpu.VMEM((8 * cap, 8 * cap), F32),
        pltpu.VMEM((ff, 8 * cap), BF16),
        pltpu.VMEM((8 * cap, dw), BF16),
        parts,
        dma((13,)), dma((LINKS,)), dma((LINKS,)),
    ]
    out = pl.pallas_call(
        functools.partial(body, (nz, ff, dw, cap, tok)),
        out_shape=jax.ShapeDtypeStruct((share * lanes, 128), F32),
        in_specs=[pl.BlockSpec(memory_space=pl.ANY)] * 6,
        out_specs=pl.BlockSpec(memory_space=pltpu.VMEM),
        scratch_shapes=scratch,
        compiler_params=pltpu.CompilerParams(
            collective_id=0, has_side_effects=True, vmem_limit_bytes=62 * 1024 * 1024
        ),
        name="clipped_grads",
    )(grad_out, routes.T, route_weight.T, example_ids, example_weight, hidden[0, 0])
    return out.reshape(share, 1, dw)


def solution(mesh):
    nz = mesh.shape["dp"] // NX
    placed = (
        P(("dp", "expert"), None),
        P(("dp", "expert"), None),
        P(("dp", "expert"), None),
        P("dp", "expert"),
        P("dp", None),
        P("dp", "expert", None, None, None),
    )
    return jax.shard_map(
        functools.partial(shards, nz), mesh=mesh, in_specs=placed,
        out_specs=P("dp", "expert", None), check_vma=False,
    )
```

```python
import functools

import jax
import jax.numpy as jnp
from jax import lax
from jax.experimental import pallas as pl
from jax.experimental.pallas import tpu as pltpu
from jax.sharding import PartitionSpec as P

EXAMPLES = 8
TOP = 6
NX = 4
MESH = pl.DeviceIdType.MESH
F32 = jnp.float32
BF16 = jnp.bfloat16

RUNS = (4, 4)
LINKS = 112
STRIDE = 5

REL = ((2, 0), (2, 1), (1, 0), (3, 0), (1, 1), (3, 1), (0, 1), (0, 0))


def nt_dot(a, b):
    return lax.dot_general(a, b, (((1,), (1,)), ((), ())), preferred_element_type=F32)


def nn_dot(a, b):
    return lax.dot_general(a, b, (((1,), (0,)), ((), ())), preferred_element_type=F32)


def iota(shape, dim):
    return lax.broadcasted_iota(jnp.int32, shape, dim)


def other(src, dst, send_sem, recv_sem, **device):
    return pltpu.make_async_remote_copy(
        src_ref=src, dst_ref=dst, send_sem=send_sem, recv_sem=recv_sem,
        device_id=device, device_id_type=MESH,
    )


def encode(value):
    most = jnp.max(jnp.abs(value), axis=0, keepdims=True)
    step = jnp.maximum(most, 1e-33) * (1.0 / 32760.0)
    code = jnp.round(value * (1.0 / step)).astype(jnp.int32)
    return code, step


def decode(code, step):
    return code.astype(jnp.int32).astype(F32) * step


def body(
    cfg,
    go_hbm, routes_hbm, weight_hbm, ids_hbm, ew_hbm, h_ref,
    out_ref,
    go_ref, routes_ref, weight_ref, ids_ref, ew_ref,
    h_buf, rank_s, scale_s, lo_s, hi_s, send_buf, relay_buf, c_buf, meta_send, meta_recv, sq_send, sq_recv,
    gl_head, gl_rest, ht_s, scaled_s, parts,
    local_sem, send_sem, recv_sem,
):
    nz, ff, dw, cap, tok = cfg
    lanes = dw // 128
    dp, me = lax.axis_index("dp"), lax.axis_index("expert")
    x, z = dp // nz, dp % nz
    y, core = me // 2, me % 2
    xp, xm, x2 = (x + 1) % NX, (x + 3) % NX, (x + 2) % NX

    def expert_at(dy, dc):
        return dict(expert=((y + dy) % 4) * 2 + (core + dc) % 2)

    def x_at(dx):
        return dict(dp=((x + dx) % NX) * nz + z)

    def z_at(dz):
        return dict(dp=x * nz + (z + nz + dz) % nz)

    dest = [expert_at(dy, dc)["expert"] for dy, dc in REL]
    source = [((y + 4 - dy) % 4) * 2 + (core + 2 - dc) % 2 for dy, dc in REL]
    copies = []

    def link(src, dst, place):
        n = len(copies)
        copies.append(other(src, dst, send_sem.at[n], recv_sem.at[n], **place))
        return copies[-1]

    inputs = [
        pltpu.make_async_copy(src, dst, local_sem.at[n])
        for n, (src, dst) in enumerate((
            (routes_hbm, routes_ref), (weight_hbm, weight_ref), (ids_hbm, ids_ref),
            (ew_hbm, ew_ref), (go_hbm, go_ref),
        ))
    ]
    for copy in inputs:
        copy.start()
    barrier = pltpu.get_barrier_semaphore()
    greeted = [expert_at(dy, dc) for dy, dc in REL[:7]]
    greeted += [x_at(dx) for dx in (1, 2, 3)] + [z_at(dz) for dz in (1, -1, 2, -2, 3, -3)]
    for place in greeted:
        pl.semaphore_signal(barrier, inc=1, device_id=place, device_id_type=MESH)

    h_copies = [
        pltpu.make_async_copy(h_ref.at[source[p]], h_buf.at[p], local_sem.at[5 + p])
        for p in range(8)
    ]
    for copy in h_copies:
        copy.start()
    for copy in inputs[:4]:
        copy.wait()

    expert_row = iota((8, tok), 0)
    routed = jnp.zeros((8, tok), F32)
    weight = jnp.zeros((8, tok), F32)
    for k in range(TOP):
        match = routes_ref[k : k + 1, :] == expert_row
        routed = jnp.where(match, 1.0, routed)
        weight = jnp.where(match, weight_ref[k : k + 1, :], weight)
    ids = ids_ref[...]
    token_weight = jnp.zeros((1, tok), F32)
    for example in range(EXAMPLES):
        token_weight = jnp.where(
            ids == example, ew_ref[0:1, example : example + 1], token_weight
        )
    earlier = (iota((tok, tok), 0) < iota((tok, tok), 1)).astype(F32).astype(BF16)
    routed_b = routed.astype(BF16)
    rank = nn_dot(routed_b, earlier)
    rank_s[...] = jnp.where(routed > 0.5, rank, -1.0)
    scale_s[...] = weight * token_weight
    example_col = iota((128, tok), 0)
    lo_s[...] = nt_dot(routed_b, (ids < example_col).astype(F32).astype(BF16))
    hi_s[...] = nt_dot(routed_b, (ids <= example_col).astype(F32).astype(BF16))

    slot_col = iota((cap, tok), 0).astype(F32)
    sub2 = iota((2, 128), 0)
    c_copies = [
        link(send_buf.at[0], relay_buf.at[0], expert_at(1, 0)),
        link(send_buf.at[1], relay_buf.at[1], expert_at(3, 0)),
    ]
    c_copies += [link(send_buf.at[p], c_buf.at[p], expert_at(*REL[p])) for p in range(2, 7)]
    relays = [
        link(relay_buf.at[0], c_buf.at[0], expert_at(1, 0)),
        link(relay_buf.at[1], c_buf.at[1], expert_at(3, 1)),
    ]
    m_copies = [link(meta_send.at[p], meta_recv.at[p], expert_at(*REL[p])) for p in range(7)]
    inputs[4].wait()
    for batch in ((0, 1), (2, 3, 4, 5), (6, 7)):
        masks, scales = [], []
        for p in batch:
            hit = rank_s[pl.ds(dest[p], 1), :] == slot_col
            masks.append(hit.astype(F32).astype(BF16))
            scales.append(
                jnp.sum(jnp.where(hit, scale_s[pl.ds(dest[p], 1), :], 0.0), axis=1, keepdims=True)
            )
        rows = nn_dot(jnp.concatenate(masks, axis=0), go_ref[...])
        if batch[0] == 0:
            pl.semaphore_wait(barrier, len(greeted))
        for i, p in enumerate(batch):
            value = (rows[i * cap : (i + 1) * cap, :] * scales[i]).astype(BF16)
            bounds = jnp.where(
                sub2 == 0, lo_s[pl.ds(dest[p], 1), :], hi_s[pl.ds(dest[p], 1), :]
            )
            if p == 7:
                c_buf[7] = value
                meta_recv[7] = bounds
            else:
                send_buf[p] = value
                meta_send[p] = bounds
                c_copies[p].start()
                m_copies[p].start()

    for copy in h_copies:
        copy.wait()
    h = h_buf[...].reshape(8 * cap, ff)
    late = 2 * cap
    head, rest = h[:late], h[late:]
    gl_head[...] = nt_dot(head, h)
    gl_rest[...] = nt_dot(rest, rest)
    share = ff // (NX * nz)
    j = iota((ff, 1), 0).astype(F32)
    unit, start, taken = j, 0, 0
    starts = []
    for n, rows in enumerate(RUNS + (share - sum(RUNS),)):
        at = j - start
        q = jnp.floor((at + 0.5) * (1.0 / rows))
        r = at - rows * q
        if n == len(RUNS):
            zq = jnp.floor((q + 0.5) * (1.0 / NX))
            xq = q - NX * zq
        else:
            xq = jnp.floor((q + 0.5) * (1.0 / nz))
            zq = q - nz * xq
        zq = STRIDE * zq
        q = nz * xq + zq - nz * jnp.floor((zq + 0.5) * (1.0 / nz))
        unit = jnp.where(j >= start, share * q + taken + r, unit)
        starts.append(start)
        start, taken = start + NX * nz * rows, taken + rows
    order = (iota((ff, ff), 1).astype(F32) == unit).astype(F32).astype(BF16)
    ht_s[...] = nt_dot(order, h).astype(BF16)

    for n in range(2):
        c_copies[n].wait_recv()
        relays[n].start()
    for p in range(7):
        m_copies[p].wait_recv()
    slot_128 = iota((cap, 128), 0).astype(F32)
    member = jnp.concatenate(
        [
            jnp.where(
                (slot_128 >= meta_recv[p, 0:1, :]) & (slot_128 < meta_recv[p, 1:2, :]), 1.0, 0.0
            )
            for p in range(8)
        ],
        axis=0,
    )
    member_b = member.astype(BF16)
    twice = jnp.where(iota((late, 8 * cap), 1) < late, 1.0, 2.0)
    gl_head[...] = gl_head[...] * (twice * nt_dot(member_b[:late], member_b))
    gl_rest[...] = gl_rest[...] * nt_dot(member_b[late:], member_b[late:])
    for p in range(2, 7):
        c_copies[p].wait_recv()
    rest = c_buf[2:8].reshape(6 * cap, dw)
    spread = jnp.sum(gl_rest[...] * nt_dot(rest, rest), axis=1, keepdims=True)
    squares = jnp.sum(member[late:] * spread, axis=0, keepdims=True)
    for copy in relays:
        copy.wait_recv()
    cot = c_buf[...].reshape(8 * cap, dw)
    spread = jnp.sum(gl_head[...] * nt_dot(cot[:late], cot), axis=1, keepdims=True)
    squares = squares + jnp.sum(member[:late] * spread, axis=0, keepdims=True)
    sq_send[...] = squares
    q_copies = [link(sq_send, sq_recv.at[p], expert_at(*REL[p])) for p in range(7)]
    for copy in q_copies:
        copy.start()
    total = squares
    for p in range(7):
        q_copies[p].wait_recv()
        total = total + sq_recv[p]
    clip = 1.0 / jnp.maximum(jnp.sqrt(total / (ff * dw)), 1.0)
    slot_weight = jnp.sum(member * clip, axis=1, keepdims=True) / EXAMPLES
    scaled_s[...] = (slot_weight * cot.astype(F32)).astype(BF16)

    half = nz // 2

    def begin(messages):
        for copy in messages:
            copy.start()

    def arrive(messages):
        for copy in messages:
            copy.wait_recv()

    def gradient(dst, start, rows):
        value = nn_dot(ht_s[pl.ds(start, rows), :], scaled_s[...])
        for n in range(lanes):
            dst[pl.ds(n, rows, stride=lanes), :] = value[:, n * 128 : (n + 1) * 128]

    class AlongX:
        def __init__(self, n):
            self.start, self.rows = starts[n], nz * RUNS[n]
            self.chunk = RUNS[n] * lanes
            self.half = half * self.chunk
            self.lower, self.upper = pl.ds(0, self.half), pl.ds(self.half, self.half)
            refs = parts[n]
            self.sums, self.z = refs["sums"], refs["z"]
            self.codes, self.steps = refs["x_codes"], refs["x_steps"]
            self.taken, self.taken_steps = refs["x_in"], refs["x_in_steps"]
            self.messages = []
            for m in range(6):
                place = x_at(1 if m % 2 == 0 else 3)
                self.messages.append([
                    link(self.steps.at[m], self.taken_steps.at[m], place),
                    link(self.codes.at[m], self.taken.at[m], place),
                ])

        def gradient(self, quarter):
            start = pl.multiple_of(self.start + quarter * self.rows, 16)
            gradient(self.sums.at[quarter], start, self.rows)

        def send(self, m, value):
            code, self.steps[m] = encode(value)
            self.codes[m] = code.astype(jnp.int16)
            begin(self.messages[m])

        def value(self, m):
            return decode(self.taken[m], self.taken_steps[m])

        def opposite(self):
            self.gradient(x2)
            self.send(0, self.sums[x2, self.lower, :])
            self.send(1, self.sums[x2, self.upper, :])

        def near(self):
            self.gradient(xp)
            self.send(2, self.sums[xp, self.upper, :])
            self.gradient(xm)
            self.send(3, self.sums[xm, self.lower, :])

        def relay(self):
            arrive(self.messages[0])
            self.send(4, self.sums[xp, self.lower, :] + self.value(0))
            arrive(self.messages[1])
            self.send(5, self.sums[xm, self.upper, :] + self.value(1))

        def finish(self):
            for m in (2, 3, 4, 5):
                arrive(self.messages[m])
            self.sums[x, self.lower, :] = self.sums[x, self.lower, :] + (self.value(4) + self.value(3))
            self.sums[x, self.upper, :] = self.sums[x, self.upper, :] + (self.value(2) + self.value(5))

        def at(self, n):
            return self.sums[x, pl.ds(pl.multiple_of(n * self.chunk, 8), self.chunk), :]

    def place(d):
        return (pow(STRIDE, -1, nz) * (z + nz + d)) % nz

    def z_start(refs, sums, rows, side):
        code, refs["steps"][0] = encode(sums)
        code = code.reshape(nz, rows, 128).astype(jnp.int16)
        refs["codes"][1 : nz + 1] = code
        refs["codes"][0] = code[nz - 1]
        refs["codes"][nz + 1] = code[0]
        started = []
        for n, o in enumerate((2, -2, 3 * side, 1, -1)):
            started.append(link(refs["steps"].at[0], refs["in_steps"].at[n], z_at(o)))
            if n == 2:
                src, dst = refs["codes"].at[1 + place(half)], refs["in_far"]
            else:
                src, dst = refs["codes"].at[pl.ds(place(o), 3)], refs["in"].at[n - n // 3]
            started.append(link(src, dst, z_at(o)))
        begin(started)
        return started

    def z_middle(refs, started, sums_at, side):
        arrive(started)
        pieces = [sums_at((place(0) + nz + d) % nz) for d in (-1, 0, 1)]
        for n in range(4):
            for m in range(3):
                pieces[m] = pieces[m] + decode(refs["in"][n, m], refs["in_steps"][n + n // 2])
        pieces[1 + side] = pieces[1 + side] + decode(refs["in_far"][...], refs["in_steps"][2])
        return pieces[1], pieces[2], pieces[0]

    def z_second(refs, pieces, rows):
        code, refs["steps"][1] = encode(jnp.concatenate(pieces[1:], axis=0))
        refs["codes2"][...] = code.reshape(2, rows, 128).astype(jnp.int16)
        refs["own"][...] = pieces[0]
        started = []
        for n, o in enumerate((5, -5)):
            started.append(link(refs["steps"].at[1], refs["in_steps"].at[5 + n], z_at(o)))
            started.append(link(refs["codes2"].at[n], refs["in2"].at[n], z_at(o)))
        begin(started)
        return started

    def z_end(refs, started):
        arrive(started)
        value = refs["own"][...]
        for n in range(2):
            value = value + decode(refs["in2"][n], refs["in_steps"][5 + n])
        return value

    refs_b = parts[-1]
    zb = refs_b["z"]
    rb = (share - sum(RUNS)) * lanes
    sums_b = refs_b["sums"]

    def b_at(n):
        return sums_b[pl.ds(pl.multiple_of(n * NX * rb, 8), NX * rb), :]

    one, two = AlongX(0), AlongX(1)
    one.opposite()
    gradient(sums_b, starts[-1], NX * nz * (rb // lanes))
    started_b = z_start(zb, sums_b[...], NX * rb, -1)
    one.near()
    two.opposite()
    one.relay()
    two.near()
    one.gradient(x)
    two.gradient(x)
    two.relay()
    one.finish()
    started_1 = z_start(one.z, one.sums[x], one.chunk, 1)
    two.finish()
    started_2 = z_start(two.z, two.sums[x], two.chunk, 1)

    pieces = z_middle(zb, started_b, b_at, -1)
    value = jnp.concatenate([p.reshape(NX, rb, 128) for p in pieces], axis=1)
    refs_b["x_own"][...] = value
    code, refs_b["x_steps"][0] = encode(value.reshape(NX * 3 * rb, 128))
    refs_b["x_codes"][...] = code.reshape(NX, 3 * rb, 128).astype(jnp.int16)
    across = []
    for n, dx in enumerate((2, 1, 3)):
        across.append(link(refs_b["x_steps"].at[0], refs_b["x_steps"].at[1 + n], x_at(dx)))
        across.append(link(refs_b["x_codes"].at[(x + dx) % NX], refs_b["x_in"].at[n], x_at(dx)))
    begin(across)

    pieces = z_middle(one.z, started_1, one.at, 1)
    started_1 = z_second(one.z, pieces, one.chunk)
    pieces = z_middle(two.z, started_2, two.at, 1)
    started_2 = z_second(two.z, pieces, two.chunk)
    arrive(across)
    value = refs_b["x_own"][x]
    for n in range(3):
        value = value + decode(refs_b["x_in"][n], refs_b["x_steps"][1 + n])
    started_b = z_second(zb, [value[n * rb : (n + 1) * rb, :] for n in range(3)], rb)
    sent = len(copies) - 12
    for copy in copies[:sent]:
        copy.wait_send()
    out_ref[0 : one.chunk, :] = z_end(one.z, started_1)
    out_ref[one.chunk : one.chunk + two.chunk, :] = z_end(two.z, started_2)
    out_ref[one.chunk + two.chunk :, :] = z_end(zb, started_b)
    for copy in copies[sent:]:
        copy.wait_send()


def shards(nz, grad_out, routes, route_weight, example_ids, example_weight, hidden):
    tok, dw = grad_out.shape
    cap, ff = hidden.shape[3:]
    lanes = dw // 128
    share = ff // (NX * nz)
    half = nz // 2
    i16 = jnp.int16

    def z_refs(rows, last):
        return dict(
            codes=pltpu.VMEM((nz + 2, rows, 128), i16),
            steps=pltpu.VMEM((2, 1, 128), F32),
            **{"in": pltpu.VMEM((4, 3, rows, 128), i16)},
            in_far=pltpu.VMEM((rows, 128), i16),
            in_steps=pltpu.VMEM((7, 1, 128), F32),
            codes2=pltpu.VMEM((2, last, 128), i16),
            in2=pltpu.VMEM((2, last, 128), i16),
            own=pltpu.VMEM((last, 128), F32),
        )

    parts = []
    for rows in RUNS:
        chunk = rows * lanes
        parts.append(dict(
            sums=pltpu.VMEM((NX, nz * chunk, 128), F32),
            x_codes=pltpu.VMEM((6, half * chunk, 128), i16),
            x_steps=pltpu.VMEM((6, 1, 128), F32),
            x_in=pltpu.VMEM((6, half * chunk, 128), i16),
            x_in_steps=pltpu.VMEM((6, 1, 128), F32),
            z=z_refs(chunk, chunk),
        ))
    rb = (share - sum(RUNS)) * lanes
    parts.append(dict(
        sums=pltpu.VMEM((nz * NX * rb, 128), F32),
        x_own=pltpu.VMEM((NX, 3 * rb, 128), F32),
        x_codes=pltpu.VMEM((NX, 3 * rb, 128), i16),
        x_in=pltpu.VMEM((3, 3 * rb, 128), i16),
        x_steps=pltpu.VMEM((4, 1, 128), F32),
        z=z_refs(NX * rb, rb),
    ))
    dma = pltpu.SemaphoreType.DMA
    scratch = [
        pltpu.VMEM((tok, dw), BF16),
        pltpu.VMEM((TOP, tok), jnp.int32),
        pltpu.VMEM((TOP, tok), F32),
        pltpu.VMEM((1, tok), jnp.int32),
        pltpu.VMEM((1, EXAMPLES), F32),
        pltpu.VMEM((8, cap, ff), BF16),
        pltpu.VMEM((8, tok), F32),
        pltpu.VMEM((8, tok), F32),
        pltpu.VMEM((8, 128), F32),
        pltpu.VMEM((8, 128), F32),
        pltpu.VMEM((7, cap, dw), BF16),
        pltpu.VMEM((2, cap, dw), BF16),
        pltpu.VMEM((8, cap, dw), BF16),
        pltpu.VMEM((7, 2, 128), F32),
        pltpu.VMEM((8, 2, 128), F32),
        pltpu.VMEM((1, 128), F32),
        pltpu.VMEM((7, 1, 128), F32),
        pltpu.VMEM((2 * cap, 8 * cap), F32),
        pltpu.VMEM((6 * cap, 6 * cap), F32),
        pltpu.VMEM((ff, 8 * cap), BF16),
        pltpu.VMEM((8 * cap, dw), BF16),
        parts,
        dma((13,)), dma((LINKS,)), dma((LINKS,)),
    ]
    out = pl.pallas_call(
        functools.partial(body, (nz, ff, dw, cap, tok)),
        out_shape=jax.ShapeDtypeStruct((share * lanes, 128), F32),
        in_specs=[pl.BlockSpec(memory_space=pl.ANY)] * 6,
        out_specs=pl.BlockSpec(memory_space=pltpu.VMEM),
        scratch_shapes=scratch,
        compiler_params=pltpu.CompilerParams(
            collective_id=0, has_side_effects=True, vmem_limit_bytes=62 * 1024 * 1024
        ),
        name="clipped_grads",
    )(grad_out, routes.T, route_weight.T, example_ids, example_weight, hidden[0, 0])
    return out.reshape(share, 1, dw)


def solution(mesh):
    nz = mesh.shape["dp"] // NX
    placed = (
        P(("dp", "expert"), None),
        P(("dp", "expert"), None),
        P(("dp", "expert"), None),
        P("dp", "expert"),
        P("dp", None),
        P("dp", "expert", None, None, None),
    )
    return jax.shard_map(
        functools.partial(shards, nz), mesh=mesh, in_specs=placed,
        out_specs=P("dp", "expert", None), check_vma=False,
    )
```
